32 devices in a mesh: tile: 8 (over z, x), chan: 4 (over y, core).
Axes of the slice: x: 2, y: 2, z: 4, core: 2. Of those that a mesh axis runs over, the one named last changes fastest.
Arguments:
- features: bfloat16 [192, 16384], P('chan', 'tile'), may hold values from -6 to 6
- pre_act: bfloat16 [192, 16384], P('chan', 'tile'), may hold values from -6 to 6
- cotangent: bfloat16 [192, 16384], P('chan', 'tile'), may hold values from -6 to 6
- weight_one: bfloat16 [27, 192, 192], P(None, 'chan'), may hold values from -0.109375 to 0.109375
- weight_two: bfloat16 [27, 192, 192], P(None, 'chan'), may hold values from -0.109375 to 0.109375
- send_list: int32 [8, 8, 4], P('tile'), may hold values from 0 to 16, as said below
- pair_in: int32 [8, 27, 16], P('tile'), may hold values from 0 to 48, as said below
- pair_out: int32 [8, 27, 16], P('tile'), may hold values from 0 to 16, as said below
Outputs:
- grad_features: bfloat16 [192, 16384], P('chan', 'tile')
- grad_weight_one: float32 [27, 192, 192], P(None, 'chan')
- grad_weight_two: float32 [27, 192, 192], P(None, 'chan')
The draws below stay inside these ranges and needn't reach their ends.
Inputs may be any that keep to these rules, and one draw needn't show every extreme that they name: send_list[t, n, :] names distinct blocks of tile t, live entries first and then 16; a direction that leaves the tile grid has only 16; the list of tile 0 for direction 6 is full. pair_out[t, k, p] is p for a live pair and 16 for an empty one; at offset 27 // 2 every pair is live. pair_in[t, k, p] is 48 exactly for empty pairs; for live pairs it is a block of tile t or an entry 16 + n * 4 + s whose list entry send_list[u, 7 - n, s] of the neighbour u in direction n is live; at offset 27 // 2 it is p.
All inputs are finite; a program needn't handle non-finite values.
Results may differ from the reference program's by a relative error of at most 0.0037.
Values may be sent and summed in bfloat16 or wider, within the bound.
No kernel may reach another device: no remote copies, remote signals or barrier semaphores. Data moves between devices by JAX's collectives and lax.ppermute only.
A program may use at most 64 MiB of HBM per device.

```python
import math
import jax
import jax.numpy as jnp
from jax import lax

C = 192
OFFSETS = 27
ROWS = 128
SLOT = 4
TILE_Y = 4
BLK_DEV = 16
VOXELS = 16384
N_TILE = 8


STEP_ROW = (-1, -1, -1, 0, 0, 1, 1, 1)


STEP_COL = (-1, 0, 1, -1, 1, -1, 0, 1)


def layout(key):
    tile_ids = jnp.arange(N_TILE, dtype=jnp.int32)
    tile_row = tile_ids // TILE_Y
    tile_col = tile_ids % TILE_Y
    near_row = tile_row[:, None] + jnp.array(STEP_ROW, dtype=jnp.int32)[None, :]
    near_col = tile_col[:, None] + jnp.array(STEP_COL, dtype=jnp.int32)[None, :]
    inside = (near_row >= 0) & (near_row < N_TILE // TILE_Y) & (near_col >= 0) & (near_col < TILE_Y)
    flat_ids = jnp.where(inside, near_row * TILE_Y + near_col, 0).astype(jnp.int32)
    counts = jax.random.randint(jax.random.fold_in(key, 101), (N_TILE, 8), 0, SLOT + 1)
    counts = jnp.where(inside, counts, 0)
    counts = counts.at[0, 6].set(SLOT)
    scores = jax.random.randint(jax.random.fold_in(key, 202), (N_TILE, 8, BLK_DEV), 0, 1 << 20)
    scores = scores * BLK_DEV + jnp.arange(BLK_DEV, dtype=jnp.int32)
    ordering = jnp.argsort(scores, axis=-1)[:, :, :SLOT].astype(jnp.int32)
    slot_ids = jnp.arange(SLOT, dtype=jnp.int32)
    send_list = jnp.where(slot_ids[None, None, :] < counts[:, :, None], ordering, BLK_DEV).astype(jnp.int32)
    opposite = (7 - jnp.arange(8, dtype=jnp.int32))[None, :]
    received = jnp.where(inside, counts[flat_ids, opposite], 0)
    level = jax.random.randint(jax.random.fold_in(key, 303), (N_TILE, 1, 1), 3, 10)
    live = jax.random.randint(jax.random.fold_in(key, 404), (N_TILE, OFFSETS, BLK_DEV), 0, 10) < level
    live = live.at[:, OFFSETS // 2, :].set(True)
    live = live.at[0, 0, 0].set(False)
    block_ids = jnp.arange(BLK_DEV, dtype=jnp.int32)[None, None, :]
    pair_out = jnp.where(live, block_ids, BLK_DEV).astype(jnp.int32)
    picked = jax.random.randint(jax.random.fold_in(key, 505), (N_TILE, OFFSETS, BLK_DEV), 0, BLK_DEV + 8 * SLOT)
    ghost_ids = picked - BLK_DEV
    direction = jnp.clip(ghost_ids // SLOT, 0, 7)
    position = ghost_ids % SLOT
    dir_count = jnp.take_along_axis(received, direction.reshape(N_TILE, -1), axis=1).reshape(N_TILE, OFFSETS, BLK_DEV)
    usable = (ghost_ids >= 0) & (position < dir_count)
    fallback = jax.random.randint(jax.random.fold_in(key, 606), (N_TILE, OFFSETS, BLK_DEV), 0, BLK_DEV)
    pair_in = jnp.where(picked < BLK_DEV, picked, jnp.where(usable, picked, fallback))
    centre = jnp.broadcast_to(jnp.arange(BLK_DEV, dtype=jnp.int32)[None, :], (N_TILE, BLK_DEV))
    pair_in = pair_in.at[:, OFFSETS // 2, :].set(centre)
    pair_in = jnp.where(live, pair_in, BLK_DEV + 8 * SLOT).astype(jnp.int32)
    return (send_list, pair_in, pair_out)


def draw_send_list(key, part):
    return layout(key)[0]


def draw_pair_in(key, part):
    return layout(key)[1]


def draw_pair_out(key, part):
    return layout(key)[2]


def steps_of(stream_key, dims, split, low, largest):
    gain = 1.0
    for dim, parts in split:
        heights = jax.random.uniform(jax.random.fold_in(jax.random.fold_in(stream_key, 6), dim), (parts,), jnp.float32, low / len(split), largest / len(split))
        gain = gain * jnp.repeat(jnp.exp(heights), dims[dim] // parts).reshape((-1,) + (1,) * (len(dims) - 1 - dim))
    return gain


def normal_values(stream_key, dims, spread, limit, cuts=(), kind=jnp.bfloat16):
    result = jax.random.normal(stream_key, dims, jnp.float32) * spread
    if len(cuts) > 0:
        result = steps_of(stream_key, dims, cuts, -0.22, 0.18) * result
    return jnp.clip(result, min=-limit, max=limit).astype(kind)


def setup_inputs(seed: int = 0) -> dict:
    key_list = jax.random.split(jax.random.key(seed), 9)
    features = normal_values(key_list[0], (C, VOXELS), 1.0, 6.0, ((0, 4), (1, 8)))
    pre_act = normal_values(key_list[1], (C, VOXELS), 1.0, 6.0, ((0, 4), (1, 8)))
    cotangent = normal_values(key_list[2], (C, VOXELS), 1.0, 6.0, ((0, 4), (1, 8)))
    weight_one = normal_values(key_list[3], (OFFSETS, C, C), (16 * C) ** -0.5, 0.109375, ((1, 4),))
    weight_two = normal_values(key_list[4], (OFFSETS, C, C), (16 * C) ** -0.5, 0.109375, ((1, 4),))
    send_list = draw_send_list(jax.random.fold_in(key_list[8], 71), 0)
    pair_in = draw_pair_in(jax.random.fold_in(key_list[8], 71), 0)
    pair_out = draw_pair_out(jax.random.fold_in(key_list[8], 71), 0)
    return {"features": features, "pre_act": pre_act, "cotangent": cotangent, "weight_one": weight_one, "weight_two": weight_two, "send_list": send_list, "pair_in": pair_in, "pair_out": pair_out}


STEP_ROW = (-1, -1, -1, 0, 0, 1, 1, 1)
STEP_COL = (-1, 0, 1, -1, 1, -1, 0, 1)

def neighbour_ids():
    tile_ids = jnp.arange(N_TILE, dtype=jnp.int32)
    tile_row = tile_ids // TILE_Y
    tile_col = tile_ids % TILE_Y
    near_row = tile_row[:, None] + jnp.array(STEP_ROW, dtype=jnp.int32)[None, :]
    near_col = tile_col[:, None] + jnp.array(STEP_COL, dtype=jnp.int32)[None, :]
    inside = (near_row >= 0) & (near_row < N_TILE // TILE_Y) & (near_col >= 0) & (near_col < TILE_Y)
    flat_ids = jnp.where(inside, near_row * TILE_Y + near_col, 0).astype(jnp.int32)
    return (inside, flat_ids)

def source_table(send_list):
    inside, flat_ids = neighbour_ids()
    nblocks = N_TILE * BLK_DEV
    tile_ids = jnp.arange(N_TILE, dtype=jnp.int32)
    local_part = tile_ids[:, None] * BLK_DEV + jnp.arange(BLK_DEV, dtype=jnp.int32)[None, :]
    opposite = (7 - jnp.arange(8, dtype=jnp.int32))[None, :]
    far_lists = send_list[flat_ids, opposite]
    far_blocks = flat_ids[:, :, None] * BLK_DEV + far_lists
    far_blocks = jnp.where(inside[:, :, None] & (far_lists < BLK_DEV), far_blocks, nblocks)
    pad_column = jnp.full((N_TILE, 1), nblocks, dtype=jnp.int32)
    table = jnp.concatenate([local_part, far_blocks.reshape(N_TILE, 8 * SLOT).astype(jnp.int32), pad_column], axis=1)
    return table.astype(jnp.int32)

def conv_back(active, grad_out, weight, table, pair_in, pair_out):
    nblocks = N_TILE * BLK_DEV
    extent = BLK_DEV + 8 * SLOT + 1
    active_pad = jnp.concatenate([active.reshape(C, nblocks, ROWS), jnp.zeros((C, 1, ROWS), active.dtype)], axis=1)
    grad_pad = jnp.concatenate([grad_out.reshape(C, nblocks, ROWS), jnp.zeros((C, 1, ROWS), grad_out.dtype)], axis=1)
    tile_ids = jnp.arange(N_TILE, dtype=jnp.int32)
    in_global = jnp.take_along_axis(table, pair_in.reshape(N_TILE, -1), axis=1).reshape(N_TILE, OFFSETS, BLK_DEV)
    out_global = jnp.where(pair_out < BLK_DEV, tile_ids[:, None, None] * BLK_DEV + pair_out, nblocks).astype(jnp.int32)
    slot_index = (tile_ids[:, None, None] * extent + pair_in).astype(jnp.int32)

    def one_offset(running, offset):
        sources = in_global[:, offset].reshape(-1)
        targets = out_global[:, offset].reshape(-1)
        places = slot_index[:, offset].reshape(-1)
        in_blocks = jnp.take(active_pad, sources, axis=1).astype(jnp.float32)
        out_blocks = jnp.take(grad_pad, targets, axis=1).astype(jnp.float32)
        weight_grad = jnp.einsum('cpr,dpr->cd', in_blocks, out_blocks)
        partial_term = jnp.einsum('cd,dpr->cpr', weight[offset].astype(jnp.float32), out_blocks)
        return (running.at[:, places].add(partial_term), weight_grad)
    initial = jnp.zeros((C, N_TILE * extent, ROWS), jnp.float32)
    running, weight_grads = lax.scan(one_offset, initial, jnp.arange(OFFSETS, dtype=jnp.int32))
    running = running.reshape(C, N_TILE, extent, ROWS)
    local_part = running[:, :, :BLK_DEV].reshape(C, nblocks, ROWS)
    ghost_part = running[:, :, BLK_DEV:BLK_DEV + 8 * SLOT].reshape(C, N_TILE * 8 * SLOT, ROWS)
    ghost_part = lax.optimization_barrier(ghost_part.astype(jnp.bfloat16)).astype(jnp.float32)
    landing = table[:, BLK_DEV:BLK_DEV + 8 * SLOT].reshape(-1)
    summed = jnp.concatenate([local_part, jnp.zeros((C, 1, ROWS), jnp.float32)], axis=1)
    summed = summed.at[:, landing].add(ghost_part)
    return (summed[:, :nblocks].reshape(C, nblocks * ROWS), weight_grads)

def reference(features, pre_act, cotangent, weight_one, weight_two, send_list, pair_in, pair_out):
    table = source_table(send_list)
    hidden = jnp.maximum(pre_act, 0)
    grad_hidden, weight_sum_two = conv_back(hidden, cotangent, weight_two, table, pair_in, pair_out)
    grad_pre = jnp.where(pre_act > 0, grad_hidden, 0.0).astype(jnp.bfloat16)
    grad_inner, weight_sum_one = conv_back(features, grad_pre, weight_one, table, pair_in, pair_out)
    grad_features = (cotangent.astype(jnp.float32) + grad_inner).astype(jnp.bfloat16)
    factor = 1.0 / math.sqrt(N_TILE * BLK_DEV * ROWS)
    return (grad_features, weight_sum_one * factor, weight_sum_two * factor)
```

```python
import functools
import math

import jax
import jax.numpy as jnp
import numpy as np
from jax import lax
from jax.experimental import pallas as pl
from jax.experimental.pallas import tpu as pltpu
from jax.sharding import PartitionSpec as P

TILE_Y = 4
STEP_ROW = (-1, -1, -1, 0, 0, 1, 1, 1)
STEP_COL = (-1, 0, 1, -1, 1, -1, 0, 1)

VMEM = pltpu.VMEM
SMEM = pltpu.SMEM
BF16 = jnp.bfloat16
F32 = jnp.float32


def vmem_spec():
    return pl.BlockSpec(memory_space=VMEM)


def smem_spec():
    return pl.BlockSpec(memory_space=SMEM)


def cost(flops, moved):
    return pl.CostEstimate(flops=flops, bytes_accessed=moved, transcendentals=0)


def ghost_plan(tile_count, block_count, slot_count):
    rows = tile_count // TILE_Y
    groups = []
    for direction in (1, 6, 3, 4, 0, 7, 2, 5):
        pairs = []
        for tile in range(tile_count):
            row = tile // TILE_Y + STEP_ROW[direction]
            col = tile % TILE_Y + STEP_COL[direction]
            if 0 <= row < rows and 0 <= col < TILE_Y:
                pairs.append((tile, row * TILE_Y + col, direction))
        for group in groups:
            sources = {p[0] for p in group}
            targets = {p[1] for p in group}
            if all(p[0] not in sources and p[1] not in targets for p in pairs):
                group.extend(pairs)
                break
        else:
            groups.append(list(pairs))
    groups = [g for g in groups if g]
    trash = block_count + 8 * slot_count + 1
    send_dir = np.zeros((len(groups), tile_count), np.int32)
    recv_base = np.full((len(groups), tile_count), trash, np.int32)
    for index, group in enumerate(groups):
        for source, target, direction in group:
            send_dir[index, source] = direction
            recv_base[index, target] = block_count + (7 - direction) * slot_count
    pair_lists = [[(s, t) for s, t, _ in g] for g in groups]
    return pair_lists, np.stack([send_dir, recv_base], axis=1)


def pack_kernel(lists_ref, plan_ref, pre_ref, feat_ref, *out_refs):
    me = lax.axis_index("tile")
    for index, out_ref in enumerate(out_refs):
        direction = plan_ref[index, 0, me]
        for slot in range(out_ref.shape[1]):
            block = jnp.minimum(lists_ref[0, direction, slot], pre_ref.shape[1] // 128 - 1)
            lanes = pl.ds(pl.multiple_of(block * 128, 128), 128)
            out_ref[0, slot] = jnp.maximum(pre_ref[:, lanes], 0)
            out_ref[1, slot] = feat_ref[:, lanes]


def pack(lists, plan, pre_act, features, slot_count):
    width = features.shape[0]
    group_count = plan.shape[0]
    shape = jax.ShapeDtypeStruct((2, slot_count, width, 128), BF16)
    return pl.pallas_call(
        pack_kernel,
        out_shape=[shape] * group_count,
        in_specs=[smem_spec(), smem_spec(), vmem_spec(), vmem_spec()],
        out_specs=[vmem_spec()] * group_count,
        name="pack_sends",
        cost_estimate=cost(0, 4 * features.size + 4 * group_count * slot_count * width * 128),
    )(lists, plan, pre_act, features)


def gather_full(parts, full):
    me = lax.axis_index("chan")
    width = parts[0].shape[0]
    for step, part in enumerate(parts):
        place = pl.multiple_of((me ^ step) * width, 16)
        full[pl.ds(place, width), :] = part[...]


def partial_kernel(group_count, pin_ref, plan_ref, *refs):
    parts, refs = refs[:4], refs[4:]
    weight_ref, local_ref = refs[:2]
    back_refs = refs[2 : 2 + group_count]
    full, product, total = refs[2 + group_count :]
    me = lax.axis_index("tile")
    offset_count, block_count = pin_ref.shape[1:]
    width = local_ref.shape[1]
    gather_full(parts, full)
    total[...] = jnp.zeros_like(total)

    def two_blocks(turn, _):
        lanes = pl.ds(pl.multiple_of(turn * 256, 256), 256)
        product[...] = jnp.dot(weight_ref[...], full[:, lanes], preferred_element_type=F32)
        for offset in range(offset_count):
            for half in range(2):
                entry = pin_ref[0, offset, turn * 2 + half]
                total[entry] += product[
                    offset * width : (offset + 1) * width, half * 128 : (half + 1) * 128
                ]
        return 0

    lax.fori_loop(0, block_count // 2, two_blocks, 0)
    local_ref[...] = total[:block_count]
    for index, back_ref in enumerate(back_refs):
        base = plan_ref[index, 1, me]
        for slot in range(back_ref.shape[0]):
            back_ref[slot] = total[base + slot].astype(BF16)


def partial_sums(pin, plan, parts, weight, slot_count):
    width, voxels = parts[0].shape
    offset_count, block_count = pin.shape[1:]
    group_count = plan.shape[0]
    entries = block_count + 9 * slot_count + 1
    outs = [jax.ShapeDtypeStruct((block_count, width, 128), F32)]
    outs += [jax.ShapeDtypeStruct((slot_count, width, 128), BF16)] * group_count
    result = pl.pallas_call(
        functools.partial(partial_kernel, group_count),
        out_shape=outs,
        in_specs=[smem_spec(), smem_spec()] + [vmem_spec()] * 5,
        out_specs=[vmem_spec()] * (1 + group_count),
        scratch_shapes=[
            VMEM((4 * width, voxels), BF16),
            VMEM((offset_count * width, 256), F32),
            VMEM((entries, width, 128), F32),
        ],
        name="partial_sums",
        cost_estimate=cost(2 * weight.size * voxels, 2 * weight.size + 12 * width * voxels),
        compiler_params=pltpu.CompilerParams(vmem_limit_bytes=24 << 20),
    )(pin, plan, *parts, weight.reshape(offset_count * width, 4 * width))
    return result[0], result[1:]


def weight_kernel(group_count, which, factor, finish, pin_ref, plan_ref, *refs):
    parts, refs = refs[:4], refs[4:]
    own_ref = refs[0]
    ghost_refs = refs[1 : 1 + group_count]
    out_count = finish.out_count
    out_refs = refs[1 + group_count : 1 + group_count + out_count]
    full, extended, gathered, *extra = refs[1 + group_count + out_count :]
    me = lax.axis_index("tile")
    offset_count, block_count = pin_ref.shape[1:]
    width = own_ref.shape[0]
    gather_full(parts, full)
    for block in range(block_count):
        value = own_ref[:, block * 128 : (block + 1) * 128]
        extended[block] = jnp.maximum(value, 0) if which == 0 else value
    for index, ghost_ref in enumerate(ghost_refs):
        base = plan_ref[index, 1, me]
        for slot in range(ghost_ref.shape[1]):
            extended[base + slot] = ghost_ref[which, slot]
    empty = block_count + 8 * ghost_refs[0].shape[1]
    extended[empty] = jnp.zeros_like(extended[empty])
    chunk = gathered.shape[0] // width

    def some_offsets(turn, _):
        for step in range(chunk):
            for block in range(block_count):
                entry = pin_ref[0, turn * chunk + step, block]
                gathered[step * width : (step + 1) * width, block * 128 : (block + 1) * 128] = (
                    extended[entry]
                )
        grads = lax.dot_general(
            gathered[...], full[...], (((1,), (1,)), ((), ())), preferred_element_type=F32
        )
        finish.store(turn, grads * factor, out_refs, extra)
        return 0

    lax.fori_loop(0, offset_count // chunk, some_offsets, 0)
    finish.end(out_refs, extra)


class PlainFinish:
    out_count = 1

    def __init__(self, rows, columns):
        self.shapes = [jax.ShapeDtypeStruct((rows, columns), F32)]
        self.scratch = []

    def store(self, turn, grads, out_refs, extra):
        rows = grads.shape[0]
        out_refs[0][pl.ds(pl.multiple_of(turn * rows, 16), rows), :] = grads

    def end(self, out_refs, extra):
        pass


def packed_rows(rows, tile_count):
    used = rows + rows // 2
    step = 16 * tile_count
    return -(-used // step) * step


class SplitFinish:
    out_count = 2

    def __init__(self, rows, columns, tile_count):
        self.rows = rows
        self.tall = packed_rows(rows, tile_count)
        half = (self.tall // 2, 128)
        self.shapes = [jax.ShapeDtypeStruct(half, F32), jax.ShapeDtypeStruct(half, BF16)]
        self.scratch = [VMEM((rows, 256), F32), VMEM((self.tall, 128), F32)]

    def store(self, turn, grads, out_refs, extra):
        rows = grads.shape[0]
        here = pl.ds(pl.multiple_of(turn * rows, 16), rows)
        extra[0][here, :192] = grads

    def end(self, out_refs, extra):
        wide, tall = extra
        rows, half = self.rows, self.rows // 2
        tall[:rows] = wide[:, :128]
        tall[rows : rows + half, :64] = wide[:half, 128:192]
        tall[rows : rows + half, 64:] = wide[half:, 128:192]
        if self.tall > rows + half:
            tall[rows + half :] = jnp.zeros((self.tall - rows - half, 128), F32)
        bit = exchange_bit(0)
        split = self.tall // 2
        out_refs[0][...] = tall[pl.ds(pl.multiple_of(bit * split, 16), split), :]
        out_refs[1][...] = tall[pl.ds(pl.multiple_of((1 - bit) * split, 16), split), :].astype(BF16)


def weight_sums(pin, plan, parts, own, ghosts, which, factor, finish):
    width, voxels = own.shape
    offset_count, block_count = pin.shape[1:]
    group_count = plan.shape[0]
    slot_count = ghosts[0].shape[1]
    entries = block_count + 9 * slot_count + 1
    chunk = 9 if offset_count % 9 == 0 else 1
    flops = 2 * offset_count * width * 4 * width * voxels
    return pl.pallas_call(
        functools.partial(weight_kernel, group_count, which, factor, finish),
        out_shape=finish.shapes,
        in_specs=[smem_spec(), smem_spec()] + [vmem_spec()] * (5 + group_count),
        out_specs=[vmem_spec()] * finish.out_count,
        scratch_shapes=[
            VMEM((4 * width, voxels), BF16),
            VMEM((entries, width, 128), BF16),
            VMEM((chunk * width, voxels), BF16),
        ]
        + finish.scratch,
        name="weight_sums",
        cost_estimate=cost(flops, 16 * width * voxels + 4 * offset_count * width * 4 * width),
        compiler_params=pltpu.CompilerParams(vmem_limit_bytes=24 << 20),
    )(pin, plan, *parts, own, *ghosts)


def settle_kernel(first, group_count, lists_ref, plan_ref, local_ref, other_ref, *refs):
    back_refs = refs[:group_count]
    out_ref, total = refs[group_count:]
    me = lax.axis_index("tile")
    block_count = local_ref.shape[0]
    total[:block_count] = local_ref[...]
    for index, back_ref in enumerate(back_refs):
        direction = plan_ref[index, 0, me]
        for slot in range(back_ref.shape[0]):
            block = lists_ref[0, direction, slot]
            total[block] += back_ref[slot].astype(F32)
    for block in range(block_count):
        lanes = slice(block * 128, (block + 1) * 128)
        other = other_ref[:, lanes].astype(F32)
        if first:
            value = jnp.where(other > 0, total[block], 0.0)
        else:
            value = other + total[block]
        out_ref[:, lanes] = value.astype(BF16)


def settle(first, lists, plan, local, other, backs):
    block_count, width, _ = local.shape
    group_count = len(backs)
    return pl.pallas_call(
        functools.partial(settle_kernel, first, group_count),
        out_shape=jax.ShapeDtypeStruct(other.shape, BF16),
        in_specs=[smem_spec(), smem_spec()] + [vmem_spec()] * (2 + group_count),
        out_specs=vmem_spec(),
        scratch_shapes=[VMEM((block_count + 1, width, 128), F32)],
        name="settle",
        cost_estimate=cost(local.size, 8 * local.size),
    )(lists, plan, local, other, *backs)


def exchange_dim(step):
    parity = lax.axis_index("chan") % 2
    if step < 2:
        return jnp.where(parity == 0, step, 1 - step)
    return step


def exchange_bit(step):
    return lax.shift_right_logical(lax.axis_index("tile"), exchange_dim(step)) & 1


def exchange_pairs(step, tile_count, chan_count):
    pairs = []
    for tile in range(tile_count):
        for chan in range(chan_count):
            dim = (1 - step if chan % 2 else step) if step < 2 else step
            pairs.append((tile * chan_count + chan, (tile ^ (1 << dim)) * chan_count + chan))
    return pairs


def halve_kernel(step, keep_ref, got_ref, next_ref, send_ref):
    bit = exchange_bit(step)
    split = next_ref.shape[0]
    mine = pl.ds(pl.multiple_of(bit * split, 16), split)
    theirs = pl.ds(pl.multiple_of((1 - bit) * split, 16), split)
    next_ref[...] = keep_ref[mine, :] + got_ref[mine, :].astype(F32)
    send_ref[...] = (keep_ref[theirs, :] + got_ref[theirs, :].astype(F32)).astype(BF16)


def halve(step, keep, got):
    rows = keep.shape[0] // 2
    return pl.pallas_call(
        functools.partial(halve_kernel, step),
        out_shape=[jax.ShapeDtypeStruct((rows, 128), F32), jax.ShapeDtypeStruct((rows, 128), BF16)],
        in_specs=[vmem_spec()] * 2,
        out_specs=[vmem_spec()] * 2,
        name="halve",
        cost_estimate=cost(keep.size, 10 * keep.size),
    )(keep, got)


def unpack_kernel(tile_count, own_ref, got_ref, out_ref, tall):
    steps = tile_count.bit_length() - 1
    chunk = tall.shape[0] // tile_count
    mine = 0
    for step in range(steps):
        mine = mine * 2 + exchange_bit(step)
    for index in range(tile_count):
        source, place = (own_ref, index) if index < tile_count // 2 else (got_ref, index - tile_count // 2)
        rows = pl.ds(pl.multiple_of((mine ^ index) * chunk, 16), chunk)
        tall[rows, :] = source[place * chunk : (place + 1) * chunk, :].astype(F32)
    rows = out_ref.shape[0]
    half = rows // 2
    out_ref[:, :128] = tall[:rows]
    out_ref[:half, 128:192] = tall[rows : rows + half, :64]
    out_ref[half:, 128:192] = tall[rows : rows + half, 64:]


def unpack(own, got, rows, columns, tile_count):
    tall = own.shape[0] * 2
    return pl.pallas_call(
        functools.partial(unpack_kernel, tile_count),
        out_shape=jax.ShapeDtypeStruct((rows, columns), F32),
        in_specs=[vmem_spec()] * 2,
        out_specs=vmem_spec(),
        scratch_shapes=[VMEM((tall, 128), F32)],
        name="unpack_sum",
        cost_estimate=cost(0, 6 * rows * columns),
    )(own, got)


def sum_over_tiles(keep, send, rows, columns):
    tile_count = lax.axis_size("tile")
    chan_count = lax.axis_size("chan")
    steps = tile_count.bit_length() - 1
    trade = lambda value, step: lax.ppermute(
        value, ("tile", "chan"), exchange_pairs(step, tile_count, chan_count)
    )
    for step in range(steps):
        got = trade(send, step)
        if step < steps - 1:
            keep, send = halve(step + 1, keep, got)
        else:
            chunk = (keep + got.astype(F32)).astype(BF16)
    for step in reversed(range(steps)):
        got = trade(chunk, step)
        if step:
            chunk = jnp.concatenate([chunk, got], axis=0)
    return unpack(chunk, got, rows, columns, tile_count)


def all_parts(part):
    trade = lambda value, bits: lax.ppermute(value, "chan", [(i, i ^ bits) for i in range(4)])
    far = trade(part, 2)
    near = trade(part, 1)
    return (part, near, far, trade(far, 1))


def shards(features, pre_act, cotangent, weight_one, weight_two, send_list, pair_in, pair_out):
    tile_count = lax.axis_size("tile")
    width, voxels = features.shape
    offset_count, _, columns = weight_one.shape
    block_count = pair_out.shape[2]
    slot_count = send_list.shape[2]
    rows = offset_count * width
    pair_lists, plan = ghost_plan(tile_count, block_count, slot_count)
    plan = jnp.asarray(plan)
    factor = 1.0 / math.sqrt(tile_count * voxels)

    sends = pack(send_list, plan, pre_act, features, slot_count)
    cot_parts = all_parts(cotangent)
    ghosts = [lax.ppermute(s, "tile", p) for s, p in zip(sends, pair_lists)]
    back_lists = [[(t, s) for s, t in p] for p in pair_lists]
    give_back = lambda backs: [lax.ppermute(b, "tile", p) for b, p in zip(backs, back_lists)]

    local_two, back_two = partial_sums(pair_in, plan, cot_parts, weight_two, slot_count)
    back_two = give_back(back_two)
    sum_two = weight_sums(
        pair_in, plan, cot_parts, pre_act, ghosts, 0, factor, PlainFinish(rows, columns)
    )[0]
    grad_two = lax.psum(sum_two, "tile")
    grad_pre = settle(True, send_list, plan, local_two, pre_act, back_two)

    pre_parts = all_parts(grad_pre)
    keep, send = weight_sums(
        pair_in, plan, pre_parts, features, ghosts, 1, factor, SplitFinish(rows, columns, tile_count)
    )
    local_one, back_one = partial_sums(pair_in, plan, pre_parts, weight_one, slot_count)
    grad_one = sum_over_tiles(keep, send, rows, columns)
    grad_features = settle(False, send_list, plan, local_one, cotangent, give_back(back_one))
    shape = (offset_count, width, columns)
    return grad_features, grad_one.reshape(shape), grad_two.reshape(shape)


def solution(mesh):
    return jax.shard_map(
        shards,
        mesh=mesh,
        in_specs=(
            P("chan", "tile"),
            P("chan", "tile"),
            P("chan", "tile"),
            P(None, "chan", None),
            P(None, "chan", None),
            P("tile", None, None),
            P("tile", None, None),
            P("tile", None, None),
        ),
        out_specs=(P("chan", "tile"), P(None, "chan", None), P(None, "chan", None)),
        check_vma=False,
    )
```

```python
import functools
import math

import jax
import jax.numpy as jnp
import numpy as np
from jax import lax
from jax.experimental import pallas as pl
from jax.experimental.pallas import tpu as pltpu
from jax.sharding import PartitionSpec as P

TILE_Y = 4
STEP_ROW = (-1, -1, -1, 0, 0, 1, 1, 1)
STEP_COL = (-1, 0, 1, -1, 1, -1, 0, 1)

VMEM = pltpu.VMEM
SMEM = pltpu.SMEM
BF16 = jnp.bfloat16
F32 = jnp.float32


def call(kernel, name, outs, smem_count, args, scratch=(), flops=0, vmem_mib=4):
    moved = sum(a.size * a.dtype.itemsize for a in args)
    moved += sum(o.size * o.dtype.itemsize for o in outs)
    return pl.pallas_call(
        kernel,
        out_shape=list(outs),
        in_specs=[pl.BlockSpec(memory_space=SMEM)] * smem_count
        + [pl.BlockSpec(memory_space=VMEM)] * (len(args) - smem_count),
        out_specs=[pl.BlockSpec(memory_space=VMEM)] * len(outs),
        scratch_shapes=list(scratch),
        name=name,
        cost_estimate=pl.CostEstimate(flops=flops, bytes_accessed=moved, transcendentals=0),
        compiler_params=pltpu.CompilerParams(vmem_limit_bytes=vmem_mib << 20),
    )(*args)


def struct(shape, dtype):
    return jax.ShapeDtypeStruct(shape, dtype)


def ghost_plan(tile_count, block_count, slot_count):
    rows = tile_count // TILE_Y

    def pairs_of(direction, keep=lambda tile: True):
        found = []
        for tile in range(tile_count):
            row = tile // TILE_Y + STEP_ROW[direction]
            col = tile % TILE_Y + STEP_COL[direction]
            if 0 <= row < rows and 0 <= col < TILE_Y and keep(tile):
                found.append((tile, row * TILE_Y + col, direction))
        return found

    groups = [
        pairs_of(4, lambda t: t % 2 == 0) + pairs_of(3, lambda t: t % 2 == 1),
        pairs_of(4, lambda t: t % 2 == 1) + pairs_of(3, lambda t: t % 2 == 0),
    ]
    for direction in (1, 6, 0, 7, 2, 5):
        pairs = pairs_of(direction)
        for group in groups[2:]:
            sources = {p[0] for p in group}
            targets = {p[1] for p in group}
            if all(p[0] not in sources and p[1] not in targets for p in pairs):
                group.extend(pairs)
                break
        else:
            groups.append(pairs)
    groups = [g for g in groups if g]
    trash = block_count + 8 * slot_count + 1
    plan = np.zeros((len(groups), 2, tile_count), np.int32)
    plan[:, 1] = trash
    for index, group in enumerate(groups):
        for source, target, direction in group:
            plan[index, 0, source] = direction
            plan[index, 1, target] = block_count + (7 - direction) * slot_count
    return [[(s, t) for s, t, _ in g] for g in groups], plan


def pack_kernel(lists_ref, plan_ref, pre_ref, feat_ref, *out_refs):
    me = lax.axis_index("tile")
    last = pre_ref.shape[1] // 128 - 1
    for index, out_ref in enumerate(out_refs):
        direction = plan_ref[index, 0, me]
        for slot in range(out_ref.shape[1]):
            block = jnp.minimum(lists_ref[0, direction, slot], last)
            lanes = pl.ds(pl.multiple_of(block * 128, 128), 128)
            out_ref[0, slot] = jnp.maximum(pre_ref[:, lanes], 0)
            out_ref[1, slot] = feat_ref[:, lanes]


def pack(lists, plan, pre_act, features):
    shape = struct((2, lists.shape[2], features.shape[0], 128), BF16)
    return call(
        pack_kernel, "pack_sends", [shape] * plan.shape[0], 2, (lists, plan, pre_act, features)
    )


def gather_full(parts, full):
    me = lax.axis_index("chan")
    width = parts[0].shape[0]
    for step, part in enumerate(parts):
        place = pl.multiple_of((me ^ step) * width, 16)
        full[pl.ds(place, width), :] = part[...]


def partial_kernel(group_count, ride_count, pin_ref, plan_ref, *refs):
    parts, refs = refs[:4], refs[4:]
    weight_ref, refs = refs[0], refs[1:]
    ride_refs, refs = refs[:ride_count], refs[ride_count:]
    local_ref = refs[0]
    back_refs = refs[1 : 1 + group_count]
    full, product, total = refs[1 + group_count :]
    me = lax.axis_index("tile")
    offset_count, block_count = pin_ref.shape[1:]
    width = local_ref.shape[1]
    gather_full(parts, full)
    total[...] = jnp.zeros_like(total)

    def two_blocks(turn, _):
        lanes = pl.ds(pl.multiple_of(turn * 256, 256), 256)
        product[...] = jnp.dot(weight_ref[...], full[:, lanes], preferred_element_type=F32)
        for offset in range(offset_count):
            for half in range(2):
                entry = pin_ref[0, offset, turn * 2 + half]
                total[entry] += product[
                    offset * width : (offset + 1) * width, half * 128 : (half + 1) * 128
                ]
        return 0

    lax.fori_loop(0, block_count // 2, two_blocks, 0)
    local_ref[...] = total[:block_count]
    for index, back_ref in enumerate(back_refs):
        base = plan_ref[index, 1, me]
        for slot in range(back_ref.shape[1]):
            back_ref[0, slot] = total[base + slot].astype(BF16)
    for ride_ref, back_ref in zip(ride_refs, back_refs):
        back_ref[1:] = ride_ref[...]


def partial_sums(pin, plan, parts, weight, slot_count, rides=()):
    width, voxels = parts[0].shape
    offset_count, block_count = pin.shape[1:]
    group_count = plan.shape[0]
    entries = block_count + 9 * slot_count + 1
    back = (slot_count, width, 128)
    outs = [struct((block_count, width, 128), F32)]
    outs += [struct((3,) + back, BF16) for _ in rides]
    outs += [struct((1,) + back, BF16)] * (group_count - len(rides))
    flat = weight.reshape(offset_count * width, 4 * width)
    result = call(
        functools.partial(partial_kernel, group_count, len(rides)),
        "partial_sums",
        outs,
        2,
        (pin, plan, *parts, flat, *rides),
        [
            VMEM((4 * width, voxels), BF16),
            VMEM((offset_count * width, 256), F32),
            VMEM((entries, width, 128), F32),
        ],
        flops=2 * weight.size * voxels,
        vmem_mib=12,
    )
    return result[0], result[1:]


def packed_rows(rows, tile_count):
    step = 16 * tile_count
    return -(-(rows + rows // 2) // step) * step


def weight_kernel(group_count, which, factor, joined, pin_ref, plan_ref, *refs):
    parts, refs = refs[:4], refs[4:]
    own_ref, refs = refs[0], refs[1:]
    ghost_refs, refs = refs[:group_count], refs[group_count:]
    other_refs, refs = refs[: 2 * joined], refs[2 * joined :]
    keep_ref, send_ref, full, extended, gathered, wide, tall = refs
    me = lax.axis_index("tile")
    offset_count, block_count = pin_ref.shape[1:]
    width = own_ref.shape[0]
    gather_full(parts, full)
    for block in range(block_count):
        value = own_ref[:, block * 128 : (block + 1) * 128]
        extended[block] = jnp.maximum(value, 0) if which == 0 else value
    for index, ghost_ref in enumerate(ghost_refs):
        base = plan_ref[index, 1, me]
        lead = ghost_ref.shape[0] - 2 + which
        for slot in range(ghost_ref.shape[1]):
            extended[base + slot] = ghost_ref[lead, slot]
    empty = block_count + 8 * ghost_refs[0].shape[1]
    extended[empty] = jnp.zeros_like(extended[empty])
    chunk = gathered.shape[0] // width

    def some_offsets(turn, _):
        for step in range(chunk):
            for block in range(block_count):
                entry = pin_ref[0, turn * chunk + step, block]
                gathered[step * width : (step + 1) * width, block * 128 : (block + 1) * 128] = (
                    extended[entry]
                )
        grads = lax.dot_general(
            gathered[...], full[...], (((1,), (1,)), ((), ())), preferred_element_type=F32
        )
        rows = chunk * width
        here = pl.ds(pl.multiple_of(turn * rows, 16), rows)
        wide[here, : grads.shape[1]] = grads * factor
        return 0

    lax.fori_loop(0, offset_count // chunk, some_offsets, 0)
    rows, half = wide.shape[0], wide.shape[0] // 2
    tall[:rows] = wide[:, :128]
    tall[rows : rows + half, :64] = wide[:half, 128:192]
    tall[rows : rows + half, 64:] = wide[half:, 128:192]
    if tall.shape[0] > rows + half:
        tall[rows + half :] = jnp.zeros((tall.shape[0] - rows - half, 128), F32)
    bit = exchange_bit(0)
    split = tall.shape[0] // 2
    if joined:
        keep_ref[:1] = other_refs[0][...]
        send_ref[:1] = other_refs[1][...]
    keep_ref[joined] = tall[pl.ds(pl.multiple_of(bit * split, 16), split), :]
    send_ref[joined] = tall[pl.ds(pl.multiple_of((1 - bit) * split, 16), split), :].astype(BF16)


def weight_sums(pin, plan, parts, own, ghosts, which, factor, tile_count, others=()):
    width, voxels = own.shape
    offset_count, block_count = pin.shape[1:]
    slot_count = ghosts[0].shape[1]
    entries = block_count + 9 * slot_count + 1
    chunk = 9 if offset_count % 9 == 0 else 1
    rows = offset_count * width
    tall = packed_rows(rows, tile_count)
    joined = 1 if others else 0
    shape = (1 + joined, tall // 2, 128)
    return call(
        functools.partial(weight_kernel, len(ghosts), which, factor, joined),
        "weight_sums",
        [struct(shape, F32), struct(shape, BF16)],
        2,
        (pin, plan, *parts, own, *ghosts, *others),
        [
            VMEM((4 * width, voxels), BF16),
            VMEM((entries, width, 128), BF16),
            VMEM((chunk * width, voxels), BF16),
            VMEM((rows, 256), F32),
            VMEM((tall, 128), F32),
        ],
        flops=2 * rows * 4 * width * voxels,
        vmem_mib=16,
    )


def settle_kernel(first, lists_ref, plan_ref, local_ref, other_ref, *refs):
    *back_refs, out_ref, total = refs
    me = lax.axis_index("tile")
    block_count = local_ref.shape[0]
    total[:block_count] = local_ref[...]
    for index, back_ref in enumerate(back_refs):
        direction = plan_ref[index, 0, me]
        for slot in range(back_ref.shape[1]):
            block = lists_ref[0, direction, slot]
            total[block] += back_ref[0, slot].astype(F32)
    for block in range(block_count):
        lanes = slice(block * 128, (block + 1) * 128)
        other = other_ref[:, lanes].astype(F32)
        if first:
            value = jnp.where(other > 0, total[block], 0.0)
        else:
            value = other + total[block]
        out_ref[:, lanes] = value.astype(BF16)


def settle(first, lists, plan, local, other, backs):
    block_count, width, _ = local.shape
    return call(
        functools.partial(settle_kernel, first),
        "settle",
        [struct(other.shape, BF16)],
        2,
        (lists, plan, local, other, *backs),
        [VMEM((block_count + 1, width, 128), F32)],
        flops=local.size,
    )[0]


def exchange_dim(step):
    parity = lax.axis_index("chan") % 2
    if step < 2:
        return jnp.where(parity == 0, step, 1 - step)
    return step


def exchange_bit(step):
    return lax.shift_right_logical(lax.axis_index("tile"), exchange_dim(step)) & 1


def trade(value, step):
    tile_count = lax.axis_size("tile")
    chan_count = lax.axis_size("chan")
    pairs = []
    for tile in range(tile_count):
        for chan in range(chan_count):
            dim = (1 - step if chan % 2 else step) if step < 2 else step
            pairs.append((tile * chan_count + chan, (tile ^ (1 << dim)) * chan_count + chan))
    return lax.ppermute(value, ("tile", "chan"), pairs)


def halve_kernel(step, keep_ref, got_ref, next_ref, send_ref):
    bit = exchange_bit(step)
    split = next_ref.shape[1]
    mine = pl.ds(pl.multiple_of(bit * split, 16), split)
    theirs = pl.ds(pl.multiple_of((1 - bit) * split, 16), split)
    for index in range(keep_ref.shape[0]):
        next_ref[index] = keep_ref[index, mine, :] + got_ref[index, mine, :].astype(F32)
        send_ref[index] = (
            keep_ref[index, theirs, :] + got_ref[index, theirs, :].astype(F32)
        ).astype(BF16)


def halve(step, keep, got):
    shape = (keep.shape[0], keep.shape[1] // 2, 128)
    return call(
        functools.partial(halve_kernel, step),
        "halve",
        [struct(shape, F32), struct(shape, BF16)],
        0,
        (keep, got),
        flops=keep.size,
    )


def unpack_kernel(tile_count, own_ref, got_ref, *refs):
    *out_refs, tall = refs
    steps = tile_count.bit_length() - 1
    chunk = own_ref.shape[2]
    mine = 0
    for step in range(steps):
        mine = mine * 2 + exchange_bit(step)
    half_count = tile_count // 2
    for part, out_ref in enumerate(out_refs):
        for index in range(tile_count):
            source = own_ref if index < half_count else got_ref
            rows = pl.ds(pl.multiple_of((mine ^ index) * chunk, 16), chunk)
            tall[rows, :] = source[index % half_count, part].astype(F32)
        rows = out_ref.shape[0]
        half = rows // 2
        out_ref[:, :128] = tall[:rows]
        out_ref[:half, 128:192] = tall[rows : rows + half, :64]
        out_ref[half:, 128:192] = tall[rows : rows + half, 64:]


def unpack(own, got, rows, columns):
    tile_count = 2 * own.shape[0]
    return call(
        functools.partial(unpack_kernel, tile_count),
        "unpack_sums",
        [struct((rows, columns), F32)] * own.shape[1],
        0,
        (own, got),
        [VMEM((tile_count * own.shape[2], 128), F32)],
        vmem_mib=8,
    )


def swap_part(value, bits):
    return lax.ppermute(value, "chan", [(i, i ^ bits) for i in range(4)])


def shards(features, pre_act, cotangent, weight_one, weight_two, send_list, pair_in, pair_out):
    tile_count = lax.axis_size("tile")
    width, voxels = features.shape
    offset_count, _, columns = weight_one.shape
    block_count = pair_out.shape[2]
    slot_count = send_list.shape[2]
    rows = offset_count * width
    steps = tile_count.bit_length() - 1
    pair_lists, plan = ghost_plan(tile_count, block_count, slot_count)
    plan = jnp.asarray(plan)
    factor = 1.0 / math.sqrt(tile_count * voxels)
    tie = lambda *values: lax.optimization_barrier(values)

    def give(values, lists):
        return [lax.ppermute(v, "tile", p) for v, p in zip(values, lists)]

    back_lists = [[(t, s) for s, t in p] for p in pair_lists]

    sends = pack(send_list, plan, pre_act, features)
    far, near = swap_part(cotangent, 2), swap_part(cotangent, 1)
    far, near, sends = tie(far, near, sends)
    cot_parts = (cotangent, near, far, swap_part(far, 1))
    ghosts = give(sends[2:], pair_lists[2:])

    local_two, backs = partial_sums(pair_in, plan, cot_parts, weight_two, slot_count, sends[:2])
    backs = give(backs, back_lists)
    backs, ghosts = tie(backs, ghosts)
    ghosts = list(backs[:2]) + list(ghosts)
    grad_pre = settle(True, send_list, plan, local_two, pre_act, backs)

    far, near = swap_part(grad_pre, 2), swap_part(grad_pre, 1)
    split_two = weight_sums(
        pair_in, plan, cot_parts, pre_act, ghosts, 0, factor, tile_count
    )
    far, near, split_two = tie(far, near, split_two)
    pre_parts = (grad_pre, near, far, swap_part(far, 1))
    keep, send = weight_sums(
        pair_in, plan, pre_parts, features, ghosts, 1, factor, tile_count, split_two
    )
    got = trade(send, 0)
    pre_parts, keep = tie(pre_parts, keep)
    local_one, backs = partial_sums(pair_in, plan, pre_parts, weight_one, slot_count)
    got, backs = tie(got, backs)
    order = list(range(2, len(backs))) + [0, 1]
    waits = 2 * steps - 2
    returned = [None] * len(backs)

    def beside(value, wait):
        share = order[wait * len(order) // waits : (wait + 1) * len(order) // waits]
        if not share:
            return value
        value, mine = tie(value, give([backs[g] for g in share], [back_lists[g] for g in share]))
        for group, back in zip(share, mine):
            returned[group] = back
        return value

    for step in range(1, steps):
        keep, send = halve(step, keep, got)
        got = beside(trade(send, step), step - 1)
    chunk = (keep + got.astype(F32)).astype(BF16)[None]
    for step in reversed(range(1, steps)):
        got = beside(trade(chunk, step), 2 * steps - 2 - step)
        chunk = jnp.concatenate([chunk, got], axis=0)
    got = trade(chunk, 0)
    grad_features = settle(False, send_list, plan, local_one, cotangent, returned)
    sum_two, sum_one = unpack(chunk, got, rows, columns)
    shape = (offset_count, width, columns)
    return grad_features, sum_one.reshape(shape), sum_two.reshape(shape)


def solution(mesh):
    return jax.shard_map(
        shards,
        mesh=mesh,
        in_specs=(
            P("chan", "tile"),
            P("chan", "tile"),
            P("chan", "tile"),
            P(None, "chan", None),
            P(None, "chan", None),
            P("tile", None, None),
            P("tile", None, None),
            P("tile", None, None),
        ),
        out_specs=(P("chan", "tile"), P(None, "chan", None), P(None, "chan", None)),
        check_vma=False,
    )
```

```python
import functools
import math

import jax
import jax.numpy as jnp
import numpy as np
from jax import lax
from jax.experimental import pallas as pl
from jax.experimental.pallas import tpu as pltpu
from jax.sharding import PartitionSpec as P

TILE_Y = 4
STEP_ROW = (-1, -1, -1, 0, 0, 1, 1, 1)
STEP_COL = (-1, 0, 1, -1, 1, -1, 0, 1)

VMEM = pltpu.VMEM
SMEM = pltpu.SMEM
BF16 = jnp.bfloat16
F32 = jnp.float32


def call(kernel, name, outs, spaces, args, scratch=(), flops=0, vmem_mib=4):
    memory = {"S": SMEM, "H": pltpu.HBM, "V": VMEM}
    spaces = spaces + "V" * (len(args) - len(spaces))
    moved = sum(a.size * a.dtype.itemsize for a in args)
    moved += sum(o.size * o.dtype.itemsize for o in outs)
    return pl.pallas_call(
        kernel,
        out_shape=list(outs),
        in_specs=[pl.BlockSpec(memory_space=memory[space]) for space in spaces],
        out_specs=[pl.BlockSpec(memory_space=VMEM)] * len(outs),
        scratch_shapes=list(scratch),
        name=name,
        cost_estimate=pl.CostEstimate(flops=flops, bytes_accessed=moved, transcendentals=0),
        compiler_params=pltpu.CompilerParams(vmem_limit_bytes=vmem_mib << 20),
    )(*(keep_in_hbm(a) if space == "H" else a for a, space in zip(args, spaces)))


def keep_in_hbm(value):
    return pltpu.with_memory_space_constraint(value, pltpu.HBM)


def struct(shape, dtype):
    return jax.ShapeDtypeStruct(shape, dtype)


def ghost_plan(tile_count, block_count, slot_count):
    rows = tile_count // TILE_Y

    def pairs_of(direction, keep=lambda tile: True):
        found = []
        for tile in range(tile_count):
            row = tile // TILE_Y + STEP_ROW[direction]
            col = tile % TILE_Y + STEP_COL[direction]
            if 0 <= row < rows and 0 <= col < TILE_Y and keep(tile):
                found.append((tile, row * TILE_Y + col, direction))
        return found

    groups = [
        pairs_of(4, lambda t: t % 2 == 0) + pairs_of(3, lambda t: t % 2 == 1),
        pairs_of(4, lambda t: t % 2 == 1) + pairs_of(3, lambda t: t % 2 == 0),
    ]
    for direction in (1, 6, 0, 7, 2, 5):
        pairs = pairs_of(direction)
        for group in groups[2:]:
            sources = {p[0] for p in group}
            targets = {p[1] for p in group}
            if all(p[0] not in sources and p[1] not in targets for p in pairs):
                group.extend(pairs)
                break
        else:
            groups.append(pairs)
    groups = [g for g in groups if g]
    trash = block_count + 8 * slot_count + 1
    plan = np.zeros((len(groups), 2, tile_count), np.int32)
    plan[:, 1] = trash
    for index, group in enumerate(groups):
        for source, target, direction in group:
            plan[index, 0, source] = direction
            plan[index, 1, target] = block_count + (7 - direction) * slot_count
    return [[(s, t) for s, t, _ in g] for g in groups], plan


def here(values):
    me = lax.axis_index("tile")
    common = int(np.bincount(values).argmax())
    found = jnp.int32(common)
    for tile, value in enumerate(values):
        if value != common:
            found = jnp.where(me == tile, jnp.int32(int(value)), found)
    return found


def pack_kernel(plan, lists_ref, *refs):
    count = plan.shape[0]
    sources, refs = refs[:4], refs[4:]
    out_refs, copied, sems = refs[:count], refs[count:-1], refs[-1]
    copies = [
        pltpu.make_async_copy(source, target, sems.at[index])
        for index, (source, target) in enumerate(zip(sources, copied))
    ]
    for copy in copies:
        copy.start()
    pre_ref, feat_ref = copied[:2]
    copies[0].wait()
    copies[1].wait()
    last = pre_ref.shape[1] // 128 - 1
    for index, out_ref in enumerate(out_refs):
        direction = here(plan[index, 0])
        for slot in range(out_ref.shape[1]):
            block = jnp.minimum(lists_ref[0, direction, slot], last)
            lanes = pl.ds(pl.multiple_of(block * 128, 128), 128)
            out_ref[0, slot] = jnp.maximum(pre_ref[:, lanes], 0)
            out_ref[1, slot] = feat_ref[:, lanes]
    copies[2].wait()
    copies[3].wait()


def pack(lists, plan, *sources):
    shape = struct((2, lists.shape[2], sources[0].shape[0], 128), BF16)
    result = call(
        functools.partial(pack_kernel, plan),
        "pack_sends",
        [shape] * plan.shape[0] + [struct(s.shape, s.dtype) for s in sources],
        "SHHHH",
        (lists, *sources),
        [pltpu.SemaphoreType.DMA((4,))],
    )
    return result[: plan.shape[0]], result[plan.shape[0] :]


def gather_full(parts, full):
    me = lax.axis_index("chan")
    width = parts[0].shape[0]
    for step, part in enumerate(parts):
        full[pl.ds(pl.multiple_of((me ^ step) * width, 16), width), :] = part[...]


def partial_kernel(plan, riders, pin_ref, weight_ref, *refs):
    group_count = plan.shape[0]
    parts, refs = refs[:4], refs[4:]
    ride_refs, refs = refs[: len(riders)], refs[len(riders) :]
    local_ref = refs[0]
    back_refs = refs[1 : 1 + group_count]
    full, even_product, odd_product, even, odd = refs[1 + group_count :]
    offset_count, block_count = pin_ref.shape[1:]
    width = local_ref.shape[1]
    gather_full(parts, full)
    even[...] = jnp.zeros_like(even)
    odd[...] = jnp.zeros_like(odd)

    def multiply(turn, product):
        lanes = pl.ds(pl.multiple_of(turn * 256, 256), 256)
        product[...] = jnp.dot(weight_ref[...], full[:, lanes], preferred_element_type=F32)

    def land(turn, product):
        for offset in range(offset_count):
            for half, total in enumerate((even, odd)):
                entry = pin_ref[0, offset, turn * 2 + half]
                total[entry] += product[
                    offset * width : (offset + 1) * width, half * 128 : (half + 1) * 128
                ]

    turns = block_count // 2
    multiply(0, even_product)

    def two_turns(step, _):
        multiply(2 * step + 1, odd_product)
        land(2 * step, even_product)
        multiply(jnp.minimum(2 * step + 2, turns - 1), even_product)
        land(2 * step + 1, odd_product)
        return 0

    lax.fori_loop(0, turns // 2, two_turns, 0)
    local_ref[...] = even[:block_count] + odd[:block_count]
    for index, back_ref in enumerate(back_refs):
        base = here(plan[index, 1])
        for slot in range(back_ref.shape[1]):
            back_ref[0, slot] = (even[base + slot] + odd[base + slot]).astype(BF16)
    for index, ride_ref in zip(riders, ride_refs):
        back_refs[index][1:] = ride_ref[...]


def partial_sums(pin, plan, parts, weight, slot_count, riders=(), rides=()):
    width, voxels = parts[0].shape
    offset_count, block_count = pin.shape[1:]
    entries = block_count + 9 * slot_count + 1
    outs = [struct((block_count, width, 128), F32)]
    for group in range(plan.shape[0]):
        outs.append(struct((3 if group in riders else 1, slot_count, width, 128), BF16))
    flat = weight.reshape(offset_count * width, 4 * width)
    result = call(
        functools.partial(partial_kernel, plan, riders),
        "partial_sums",
        outs,
        "S",
        (pin, flat, *parts, *rides),
        [
            VMEM((4 * width, voxels), BF16),
            VMEM((offset_count * width, 256), F32),
            VMEM((offset_count * width, 256), F32),
            VMEM((entries, width, 128), F32),
            VMEM((entries, width, 128), F32),
        ],
        flops=2 * weight.size * voxels,
        vmem_mib=12,
    )
    return result[0], result[1:]


def packed_rows(rows, tile_count):
    step = 16 * tile_count
    return -(-(rows + rows // 2) // step) * step


def weight_kernel(plan, which, factor, pin_ref, own_ref, *refs):
    parts, refs = refs[:4], refs[4:]
    ghost_refs, refs = refs[: plan.shape[0]], refs[plan.shape[0] :]
    keep_ref, send_ref, full, extended, gathered, wide, tall = refs
    offset_count, block_count = pin_ref.shape[1:]
    width = own_ref.shape[0]
    gather_full(parts, full)
    for block in range(block_count):
        value = own_ref[:, block * 128 : (block + 1) * 128]
        extended[block] = jnp.maximum(value, 0) if which == 0 else value
    for index, ghost_ref in enumerate(ghost_refs):
        base = here(plan[index, 1])
        for slot in range(ghost_ref.shape[1]):
            extended[base + slot] = ghost_ref[ghost_ref.shape[0] - 2 + which, slot]
    empty = block_count + 8 * ghost_refs[0].shape[1]
    extended[empty] = jnp.zeros_like(extended[empty])
    chunk = gathered.shape[0] // width

    def some_offsets(turn, _):
        for step in range(chunk):
            for block in range(block_count):
                entry = pin_ref[0, turn * chunk + step, block]
                gathered[step * width : (step + 1) * width, block * 128 : (block + 1) * 128] = (
                    extended[entry]
                )
        grads = lax.dot_general(
            gathered[...], full[...], (((1,), (1,)), ((), ())), preferred_element_type=F32
        )
        rows = chunk * width
        wide[pl.ds(pl.multiple_of(turn * rows, 16), rows), : grads.shape[1]] = grads * factor
        return 0

    lax.fori_loop(0, offset_count // chunk, some_offsets, 0)
    rows, half = wide.shape[0], wide.shape[0] // 2
    tall[:rows] = wide[:, :128]
    tall[rows : rows + half, :64] = wide[:half, 128:192]
    tall[rows : rows + half, 64:] = wide[half:, 128:192]
    if tall.shape[0] > rows + half:
        tall[rows + half :] = jnp.zeros((tall.shape[0] - rows - half, 128), F32)
    bit = exchange_bit(0)
    split = tall.shape[0] // 2
    keep_ref[...] = tall[pl.ds(pl.multiple_of(bit * split, 16), split), :]
    send_ref[...] = tall[pl.ds(pl.multiple_of((1 - bit) * split, 16), split), :].astype(BF16)


def weight_sums(pin, plan, parts, own, ghosts, which, factor, tile_count):
    width, voxels = own.shape
    offset_count, block_count = pin.shape[1:]
    slot_count = ghosts[0].shape[1]
    entries = block_count + 9 * slot_count + 1
    chunk = 9 if offset_count % 9 == 0 else 1
    rows = offset_count * width
    tall = packed_rows(rows, tile_count)
    shape = (tall // 2, 128)
    return call(
        functools.partial(weight_kernel, plan, which, factor),
        "weight_sums",
        [struct(shape, F32), struct(shape, BF16)],
        "S",
        (pin, own, *parts, *ghosts),
        [
            VMEM((4 * width, voxels), BF16),
            VMEM((entries, width, 128), BF16),
            VMEM((chunk * width, voxels), BF16),
            VMEM((rows, 256), F32),
            VMEM((tall, 128), F32),
        ],
        flops=2 * rows * 4 * width * voxels,
        vmem_mib=14,
    )


def settle_kernel(plan, first, lists_ref, other_ref, local_ref, *refs):
    *back_refs, out_ref, total = refs
    block_count = local_ref.shape[0]
    total[:block_count] = local_ref[...]
    for index, back_ref in enumerate(back_refs):
        direction = here(plan[index, 0])
        for slot in range(back_ref.shape[1]):
            block = lists_ref[0, direction, slot]
            total[block] += back_ref[0, slot].astype(F32)
    for block in range(block_count):
        lanes = slice(block * 128, (block + 1) * 128)
        other = other_ref[:, lanes].astype(F32)
        if first:
            value = jnp.where(other > 0, total[block], 0.0)
        else:
            value = other + total[block]
        out_ref[:, lanes] = value.astype(BF16)


def settle(first, lists, plan, local, other, backs):
    block_count, width, _ = local.shape
    return call(
        functools.partial(settle_kernel, plan, first),
        "settle",
        [struct(other.shape, BF16)],
        "S",
        (lists, other, local, *backs),
        [VMEM((block_count + 1, width, 128), F32)],
        flops=local.size,
    )[0]


def exchange_dim(step):
    parity = lax.axis_index("chan") % 2
    if step < 2:
        return jnp.where(parity == 0, step, 1 - step)
    return step


def exchange_bit(step):
    return lax.shift_right_logical(lax.axis_index("tile"), exchange_dim(step)) & 1


def trade(value, step):
    tile_count = lax.axis_size("tile")
    chan_count = lax.axis_size("chan")
    pairs = []
    for tile in range(tile_count):
        for chan in range(chan_count):
            dim = (1 - step if chan % 2 else step) if step < 2 else step
            pairs.append((tile * chan_count + chan, (tile ^ (1 << dim)) * chan_count + chan))
    return lax.ppermute(value, ("tile", "chan"), pairs)


def halve_kernel(step, *refs):
    *pair_refs, next_ref, send_ref = refs
    bit = exchange_bit(step)
    split = next_ref.shape[1]
    mine = pl.ds(pl.multiple_of(bit * split, 16), split)
    theirs = pl.ds(pl.multiple_of((1 - bit) * split, 16), split)
    for index in range(2):
        if len(pair_refs) == 4:
            keep, got = pair_refs[2 * index : 2 * index + 2]
        else:
            keep, got = (ref.at[index] for ref in pair_refs)
        next_ref[index] = keep[mine, :] + got[mine, :].astype(F32)
        send_ref[index] = (keep[theirs, :] + got[theirs, :].astype(F32)).astype(BF16)


def halve(step, *pairs):
    shape = (2, pairs[0].shape[-2] // 2, 128)
    return call(
        functools.partial(halve_kernel, step),
        "halve",
        [struct(shape, F32), struct(shape, BF16)],
        "",
        pairs,
        flops=2 * pairs[0].size,
    )


def unpack_kernel(tile_count, own_ref, got_ref, *refs):
    *out_refs, tall = refs
    steps = tile_count.bit_length() - 1
    chunk = own_ref.shape[2]
    mine = 0
    for step in range(steps):
        mine = mine * 2 + exchange_bit(step)
    half_count = tile_count // 2
    for part, out_ref in enumerate(out_refs):
        for index in range(tile_count):
            source = own_ref if index < half_count else got_ref
            rows = pl.ds(pl.multiple_of((mine ^ index) * chunk, 16), chunk)
            tall[rows, :] = source[index % half_count, part].astype(F32)
        rows = out_ref.shape[0]
        half = rows // 2
        out_ref[:, :128] = tall[:rows]
        out_ref[:half, 128:192] = tall[rows : rows + half, :64]
        out_ref[half:, 128:192] = tall[rows : rows + half, 64:]


def unpack(own, got, rows, columns):
    tile_count = 2 * own.shape[0]
    return call(
        functools.partial(unpack_kernel, tile_count),
        "unpack_sums",
        [struct((rows, columns), F32)] * own.shape[1],
        "",
        (own, got),
        [VMEM((tile_count * own.shape[2], 128), F32)],
        vmem_mib=8,
    )


def swap_part(value, bits):
    return lax.ppermute(value, "chan", [(i, i ^ bits) for i in range(4)])


def shards(features, pre_act, cotangent, weight_one, weight_two, send_list, pair_in, pair_out):
    tile_count = lax.axis_size("tile")
    width, voxels = features.shape
    offset_count, _, columns = weight_one.shape
    block_count = pair_out.shape[2]
    slot_count = send_list.shape[2]
    rows = offset_count * width
    steps = tile_count.bit_length() - 1
    pair_lists, plan = ghost_plan(tile_count, block_count, slot_count)
    factor = 1.0 / math.sqrt(tile_count * voxels)
    tie = lambda *values: lax.optimization_barrier(values)

    def give(values, lists):
        return [lax.ppermute(v, "tile", p) for v, p in zip(values, lists)]

    back_lists = [[(t, s) for s, t in p] for p in pair_lists]

    early = range(2, min(4, len(pair_lists)))
    riders = [g for g in range(len(pair_lists)) if g not in early]

    far, near, last = (swap_part(cotangent, bits) for bits in (2, 1, 3))
    sends, here_now = pack(send_list, plan, pre_act, features, cotangent, weight_two)
    pre_act, features, cotangent, weight_two = here_now
    soon = give([sends[g] for g in early], [pair_lists[g] for g in early])
    cot_parts = (cotangent, near, far, last)
    local_two, backs = partial_sums(
        pair_in, plan, cot_parts, weight_two, slot_count, riders, [sends[g] for g in riders]
    )
    backs, soon = tie(give(backs, back_lists), soon)
    grad_pre = settle(True, send_list, plan, local_two, pre_act, backs)

    ghosts = list(backs)
    for group, ghost in zip(early, soon):
        ghosts[group] = ghost
    far, near = swap_part(grad_pre, 2), swap_part(grad_pre, 1)
    keep_two, send = weight_sums(pair_in, plan, cot_parts, pre_act, ghosts, 0, factor, tile_count)
    far, near, send = tie(far, near, send)
    got_two = trade(send, 0)
    pre_parts = (grad_pre, near, far, swap_part(far, 1))
    keep_one, send = weight_sums(
        pair_in, plan, pre_parts, features, ghosts, 1, factor, tile_count
    )
    got_two, send = tie(got_two, send)
    got = trade(send, 0)
    pre_parts, keep_one = tie(pre_parts, keep_one)
    local_one, backs = partial_sums(pair_in, plan, pre_parts, weight_one, slot_count)
    got, backs = tie(got, backs)
    shares = [[0, 1]] + [[g] for g in range(2, len(backs))]
    returned = [None] * len(backs)

    def beside(value, step):
        share = shares.pop(0) if shares else []
        value, mine = tie(value, [backs[g] for g in share])
        got, landed = tie(trade(value, step), give(mine, [back_lists[g] for g in share]))
        for group, back in zip(share, landed):
            returned[group] = back
        return got

    arrived = (keep_two, got_two, keep_one, got)
    for step in range(1, steps):
        keep, send = halve(step, *arrived)
        got = beside(send, step)
        arrived = (keep, got)
    chunk = (keep + got.astype(F32)).astype(BF16)[None]
    for step in reversed(range(1, steps)):
        got = beside(chunk, step)
        chunk = jnp.concatenate([chunk, got], axis=0)
    got = trade(chunk, 0)
    grad_features = settle(False, send_list, plan, local_one, cotangent, returned)
    sum_two, sum_one = unpack(chunk, got, rows, columns)
    shape = (offset_count, width, columns)
    return grad_features, sum_one.reshape(shape), sum_two.reshape(shape)


def solution(mesh):
    return jax.shard_map(
        shards,
        mesh=mesh,
        in_specs=(
            P("chan", "tile"),
            P("chan", "tile"),
            P("chan", "tile"),
            P(None, "chan", None),
            P(None, "chan", None),
            P("tile", None, None),
            P("tile", None, None),
            P("tile", None, None),
        ),
        out_specs=(P("chan", "tile"), P(None, "chan", None), P(None, "chan", None)),
        check_vma=False,
    )
```

```python
import functools
import math

import jax
import jax.numpy as jnp
import numpy as np
from jax import lax
from jax.experimental import pallas as pl
from jax.experimental.pallas import tpu as pltpu
from jax.sharding import PartitionSpec as P

TILE_Y = 4
STEP_ROW = (-1, -1, -1, 0, 0, 1, 1, 1)
STEP_COL = (-1, 0, 1, -1, 1, -1, 0, 1)

VMEM = pltpu.VMEM
SMEM = pltpu.SMEM
BF16 = jnp.bfloat16
F32 = jnp.float32


def call(kernel, name, outs, spaces, args, scratch=(), flops=0, vmem_mib=4):
    memory = {"S": SMEM, "H": pltpu.HBM, "V": VMEM}
    spaces = spaces + "V" * (len(args) - len(spaces))
    moved = sum(a.size * a.dtype.itemsize for a in args)
    moved += sum(o.size * o.dtype.itemsize for o in outs)
    return pl.pallas_call(
        kernel,
        out_shape=list(outs),
        in_specs=[pl.BlockSpec(memory_space=memory[space]) for space in spaces],
        out_specs=[pl.BlockSpec(memory_space=VMEM)] * len(outs),
        scratch_shapes=list(scratch),
        name=name,
        cost_estimate=pl.CostEstimate(flops=flops, bytes_accessed=moved, transcendentals=0),
        compiler_params=pltpu.CompilerParams(vmem_limit_bytes=vmem_mib << 20),
    )(*(keep_in_hbm(a) if space == "H" else a for a, space in zip(args, spaces)))


def keep_in_hbm(value):
    return pltpu.with_memory_space_constraint(value, pltpu.HBM)


def struct(shape, dtype):
    return jax.ShapeDtypeStruct(shape, dtype)


def ghost_plan(tile_count, block_count, slot_count):
    rows = tile_count // TILE_Y

    def pairs_of(direction, keep=lambda tile: True):
        found = []
        for tile in range(tile_count):
            row = tile // TILE_Y + STEP_ROW[direction]
            col = tile % TILE_Y + STEP_COL[direction]
            if 0 <= row < rows and 0 <= col < TILE_Y and keep(tile):
                found.append((tile, row * TILE_Y + col, direction))
        return found

    groups = [
        pairs_of(4, lambda t: t % 2 == 0) + pairs_of(3, lambda t: t % 2 == 1),
        pairs_of(4, lambda t: t % 2 == 1) + pairs_of(3, lambda t: t % 2 == 0),
    ]
    for direction in (1, 6, 0, 7, 2, 5):
        pairs = pairs_of(direction)
        for group in groups[2:]:
            sources = {p[0] for p in group}
            targets = {p[1] for p in group}
            if all(p[0] not in sources and p[1] not in targets for p in pairs):
                group.extend(pairs)
                break
        else:
            groups.append(pairs)
    groups = [g for g in groups if g]
    trash = block_count + 8 * slot_count + 1
    plan = np.zeros((len(groups), 2, tile_count), np.int32)
    plan[:, 1] = trash
    for index, group in enumerate(groups):
        for source, target, direction in group:
            plan[index, 0, source] = direction
            plan[index, 1, target] = block_count + (7 - direction) * slot_count
    return [[(s, t) for s, t, _ in g] for g in groups], plan


def here(values):
    me = lax.axis_index("tile")
    common = int(np.bincount(values).argmax())
    found = jnp.int32(common)
    for tile, value in enumerate(values):
        if value != common:
            found = jnp.where(me == tile, jnp.int32(int(value)), found)
    return found


def pack_kernel(plan, lists_ref, *refs):
    count = plan.shape[0]
    sources, refs = refs[:4], refs[4:]
    out_refs, copied, sems = refs[:count], refs[count:-1], refs[-1]
    copies = [
        pltpu.make_async_copy(source, target, sems.at[index])
        for index, (source, target) in enumerate(zip(sources, copied))
    ]
    for copy in copies:
        copy.start()
    pre_ref, feat_ref = copied[:2]
    copies[0].wait()
    copies[1].wait()
    last = pre_ref.shape[1] // 128 - 1
    for index, out_ref in enumerate(out_refs):
        direction = here(plan[index, 0])
        for slot in range(out_ref.shape[1]):
            block = jnp.minimum(lists_ref[0, direction, slot], last)
            lanes = pl.ds(pl.multiple_of(block * 128, 128), 128)
            out_ref[0, slot] = jnp.maximum(pre_ref[:, lanes], 0)
            out_ref[1, slot] = feat_ref[:, lanes]
    copies[2].wait()
    copies[3].wait()


def pack(lists, plan, *sources):
    shape = struct((2, lists.shape[2], sources[0].shape[0], 128), BF16)
    result = call(
        functools.partial(pack_kernel, plan),
        "pack_sends",
        [shape] * plan.shape[0] + [struct(s.shape, s.dtype) for s in sources],
        "SHHHH",
        (lists, *sources),
        [pltpu.SemaphoreType.DMA((4,))],
    )
    return result[: plan.shape[0]], result[plan.shape[0] :]


def gather_full(parts, full):
    me = lax.axis_index("chan")
    width = parts[0].shape[0]
    for step, part in enumerate(parts):
        full[pl.ds(pl.multiple_of((me ^ step) * width, 16), width), :] = part[...]


def partial_kernel(plan, riders, pin_ref, weight_ref, *refs):
    group_count = plan.shape[0]
    parts, refs = refs[:4], refs[4:]
    ride_refs, refs = refs[: len(riders)], refs[len(riders) :]
    local_ref = refs[0]
    back_refs = refs[1 : 1 + group_count]
    full, even_product, odd_product, even, odd = refs[1 + group_count :]
    offset_count, block_count = pin_ref.shape[1:]
    width = local_ref.shape[1]
    gather_full(parts, full)
    even[...] = jnp.zeros_like(even)
    odd[...] = jnp.zeros_like(odd)

    def multiply(turn, product):
        lanes = pl.ds(pl.multiple_of(turn * 256, 256), 256)
        product[...] = jnp.dot(weight_ref[...], full[:, lanes], preferred_element_type=F32)

    def land(turn, product):
        for offset in range(offset_count):
            for half, total in enumerate((even, odd)):
                entry = pin_ref[0, offset, turn * 2 + half]
                total[entry] += product[
                    offset * width : (offset + 1) * width, half * 128 : (half + 1) * 128
                ]

    turns = block_count // 2
    multiply(0, even_product)

    def two_turns(step, _):
        multiply(2 * step + 1, odd_product)
        land(2 * step, even_product)
        multiply(jnp.minimum(2 * step + 2, turns - 1), even_product)
        land(2 * step + 1, odd_product)
        return 0

    lax.fori_loop(0, turns // 2, two_turns, 0)
    local_ref[...] = even[:block_count] + odd[:block_count]
    for index, back_ref in enumerate(back_refs):
        base = here(plan[index, 1])
        for slot in range(back_ref.shape[1]):
            back_ref[0, slot] = (even[base + slot] + odd[base + slot]).astype(BF16)
    for index, ride_ref in zip(riders, ride_refs):
        back_refs[index][1:] = ride_ref[...]


def partial_sums(pin, plan, parts, weight, slot_count, riders=(), rides=()):
    width, voxels = parts[0].shape
    offset_count, block_count = pin.shape[1:]
    entries = block_count + 9 * slot_count + 1
    outs = [struct((block_count, width, 128), F32)]
    for group in range(plan.shape[0]):
        outs.append(struct((3 if group in riders else 1, slot_count, width, 128), BF16))
    flat = weight.reshape(offset_count * width, 4 * width)
    result = call(
        functools.partial(partial_kernel, plan, riders),
        "partial_sums",
        outs,
        "S",
        (pin, flat, *parts, *rides),
        [
            VMEM((4 * width, voxels), BF16),
            VMEM((offset_count * width, 256), F32),
            VMEM((offset_count * width, 256), F32),
            VMEM((entries, width, 128), F32),
            VMEM((entries, width, 128), F32),
        ],
        flops=2 * weight.size * voxels,
        vmem_mib=12,
    )
    return result[0], result[1:]


def packed_rows(rows, tile_count):
    step = 16 * tile_count
    return -(-(rows + rows // 2) // step) * step


def weight_kernel(plan, which, factor, pieces, pin_ref, own_ref, *refs):
    parts, refs = refs[:4], refs[4:]
    ghost_refs, refs = refs[: plan.shape[0]], refs[plan.shape[0] :]
    piece_refs, refs = refs[:pieces], refs[pieces:]
    full, extended, gathered, wide, tall = refs
    offset_count, block_count = pin_ref.shape[1:]
    width = own_ref.shape[0]
    gather_full(parts, full)
    for block in range(block_count):
        value = own_ref[:, block * 128 : (block + 1) * 128]
        extended[block] = jnp.maximum(value, 0) if which == 0 else value
    for index, ghost_ref in enumerate(ghost_refs):
        base = here(plan[index, 1])
        for slot in range(ghost_ref.shape[1]):
            extended[base + slot] = ghost_ref[ghost_ref.shape[0] - 2 + which, slot]
    empty = block_count + 8 * ghost_refs[0].shape[1]
    extended[empty] = jnp.zeros_like(extended[empty])
    chunk = gathered.shape[0] // width

    def some_offsets(turn, _):
        for step in range(chunk):
            for block in range(block_count):
                entry = pin_ref[0, turn * chunk + step, block]
                gathered[step * width : (step + 1) * width, block * 128 : (block + 1) * 128] = (
                    extended[entry]
                )
        grads = lax.dot_general(
            gathered[...], full[...], (((1,), (1,)), ((), ())), preferred_element_type=F32
        )
        rows = chunk * width
        wide[pl.ds(pl.multiple_of(turn * rows, 16), rows), : grads.shape[1]] = grads * factor
        return 0

    lax.fori_loop(0, offset_count // chunk, some_offsets, 0)
    rows, half = wide.shape[0], wide.shape[0] // 2
    tall[:rows] = wide[:, :128]
    tall[rows : rows + half, :64] = wide[:half, 128:192]
    tall[rows : rows + half, 64:] = wide[half:, 128:192]
    if tall.shape[0] > rows + half:
        tall[rows + half :] = jnp.zeros((tall.shape[0] - rows - half, 128), F32)
    split = tall.shape[0] // pieces
    mine = exchange_bit(0) if pieces == 2 else 2 * exchange_bit(0) + exchange_bit(1)
    for index, piece_ref in enumerate(piece_refs):
        piece = tall[pl.ds(pl.multiple_of((mine ^ index) * split, 16), split), :]
        piece_ref[...] = piece.astype(piece_ref.dtype)


def weight_sums(pin, plan, parts, own, ghosts, which, factor, tile_count, pieces):
    width, voxels = own.shape
    offset_count, block_count = pin.shape[1:]
    slot_count = ghosts[0].shape[1]
    entries = block_count + 9 * slot_count + 1
    chunk = 9 if offset_count % 9 == 0 else 1
    rows = offset_count * width
    tall = packed_rows(rows, tile_count)
    shape = (tall // pieces, 128)
    return call(
        functools.partial(weight_kernel, plan, which, factor, pieces),
        "weight_sums",
        [struct(shape, F32)] + [struct(shape, BF16)] * (pieces - 1),
        "S",
        (pin, own, *parts, *ghosts),
        [
            VMEM((4 * width, voxels), BF16),
            VMEM((entries, width, 128), BF16),
            VMEM((chunk * width, voxels), BF16),
            VMEM((rows, 256), F32),
            VMEM((tall, 128), F32),
        ],
        flops=2 * rows * 4 * width * voxels,
        vmem_mib=14,
    )


def settle_kernel(plan, first, lists_ref, other_ref, local_ref, *refs):
    *back_refs, out_ref, total = refs
    block_count = local_ref.shape[0]
    total[:block_count] = local_ref[...]
    for index, back_ref in enumerate(back_refs):
        direction = here(plan[index, 0])
        for slot in range(back_ref.shape[1]):
            block = lists_ref[0, direction, slot]
            total[block] += back_ref[0, slot].astype(F32)
    for block in range(block_count):
        lanes = slice(block * 128, (block + 1) * 128)
        other = other_ref[:, lanes].astype(F32)
        if first:
            value = jnp.where(other > 0, total[block], 0.0)
        else:
            value = other + total[block]
        out_ref[:, lanes] = value.astype(BF16)


def settle(first, lists, plan, local, other, backs):
    block_count, width, _ = local.shape
    return call(
        functools.partial(settle_kernel, plan, first),
        "settle",
        [struct(other.shape, BF16)],
        "S",
        (lists, other, local, *backs),
        [VMEM((block_count + 1, width, 128), F32)],
        flops=local.size,
    )[0]


def exchange_dim(step):
    parity = lax.axis_index("chan") % 2
    if step < 2:
        return jnp.where(parity == 0, step, 1 - step)
    return step


def exchange_bit(step):
    return lax.shift_right_logical(lax.axis_index("tile"), exchange_dim(step)) & 1


def trade(value, *steps):
    tile_count = lax.axis_size("tile")
    chan_count = lax.axis_size("chan")
    pairs = []
    for tile in range(tile_count):
        for chan in range(chan_count):
            dims = [(1 - step if chan % 2 else step) if step < 2 else step for step in steps]
            other = tile ^ sum(1 << dim for dim in dims)
            pairs.append((tile * chan_count + chan, other * chan_count + chan))
    return lax.ppermute(value, ("tile", "chan"), pairs)


def halve_kernel(step, sources, *refs):
    *_, next_ref, send_ref = refs
    bit = exchange_bit(step)
    split = next_ref.shape[1]
    mine = pl.ds(pl.multiple_of(bit * split, 16), split)
    theirs = pl.ds(pl.multiple_of((1 - bit) * split, 16), split)
    for index, terms in enumerate(sources):
        views = [refs[term] if part is None else refs[term].at[part] for term, part in terms]
        next_ref[index] = sum(view[mine, :].astype(F32) for view in views)
        send_ref[index] = sum(view[theirs, :].astype(F32) for view in views).astype(BF16)


def halve(step, sources, *args):
    shape = (len(sources), args[0].shape[-2] // 2, 128)
    return call(
        functools.partial(halve_kernel, step, sources),
        "halve",
        [struct(shape, F32), struct(shape, BF16)],
        "",
        args,
        flops=2 * args[0].size,
    )


def merge_kernel(keep_ref, got_ref, other_ref, next_ref, send_ref):
    bit = exchange_bit(1)
    split = next_ref.shape[0]
    mine = pl.ds(pl.multiple_of(bit * split, 16), split)
    theirs = pl.ds(pl.multiple_of((1 - bit) * split, 16), split)
    next_ref[...] = keep_ref[mine, :] + got_ref[mine, :].astype(F32)
    send_ref[0] = (keep_ref[theirs, :] + got_ref[theirs, :].astype(F32)).astype(BF16)
    send_ref[1] = other_ref[...]


def merge(keep, got, other):
    return call(
        merge_kernel,
        "merge_sends",
        [struct(other.shape, F32), struct((2,) + other.shape, BF16)],
        "",
        (keep, got, other),
        flops=keep.size,
    )


def unpack_kernel(tile_count, *refs):
    quarters, out_refs, tall = refs[:4], refs[4:-1], refs[-1]
    steps = tile_count.bit_length() - 1
    count, _, chunk, _ = quarters[0].shape
    mine = 0
    for step in range(steps):
        mine = mine * 2 + exchange_bit(step)
    for part, out_ref in enumerate(out_refs):
        for index in range(tile_count):
            rows = pl.ds(pl.multiple_of((mine ^ index) * chunk, 16), chunk)
            tall[rows, :] = quarters[index // count][index % count, part].astype(F32)
        rows = out_ref.shape[0]
        half = rows // 2
        out_ref[:, :128] = tall[:rows]
        out_ref[:half, 128:192] = tall[rows : rows + half, :64]
        out_ref[half:, 128:192] = tall[rows : rows + half, 64:]


def unpack(quarters, rows, columns):
    tile_count = 4 * quarters[0].shape[0]
    return call(
        functools.partial(unpack_kernel, tile_count),
        "unpack_sums",
        [struct((rows, columns), F32)] * quarters[0].shape[1],
        "",
        quarters,
        [VMEM((tile_count * quarters[0].shape[2], 128), F32)],
        vmem_mib=8,
    )


def swap_part(value, bits):
    return lax.ppermute(value, "chan", [(i, i ^ bits) for i in range(4)])


def shards(features, pre_act, cotangent, weight_one, weight_two, send_list, pair_in, pair_out):
    tile_count = lax.axis_size("tile")
    width, voxels = features.shape
    offset_count, _, columns = weight_one.shape
    block_count = pair_out.shape[2]
    slot_count = send_list.shape[2]
    rows = offset_count * width
    steps = tile_count.bit_length() - 1
    pair_lists, plan = ghost_plan(tile_count, block_count, slot_count)
    factor = 1.0 / math.sqrt(tile_count * voxels)
    tie = lambda *values: lax.optimization_barrier(values)

    def give(values, lists):
        return [lax.ppermute(v, "tile", p) for v, p in zip(values, lists)]

    back_lists = [[(t, s) for s, t in p] for p in pair_lists]

    early = range(2, min(4, len(pair_lists)))
    riders = [g for g in range(len(pair_lists)) if g not in early]

    far, near, last = (swap_part(cotangent, bits) for bits in (2, 1, 3))
    sends, here_now = pack(send_list, plan, pre_act, features, cotangent, weight_two)
    pre_act, features, cotangent, weight_two = here_now
    soon = give([sends[g] for g in early], [pair_lists[g] for g in early])
    cot_parts = (cotangent, near, far, last)
    local_two, backs = partial_sums(
        pair_in, plan, cot_parts, weight_two, slot_count, riders, [sends[g] for g in riders]
    )
    backs, soon = tie(give(backs, back_lists), soon)
    grad_pre = settle(True, send_list, plan, local_two, pre_act, backs)

    ghosts = list(backs)
    for group, ghost in zip(early, soon):
        ghosts[group] = ghost
    far, near = swap_part(grad_pre, 2), swap_part(grad_pre, 1)
    keep_two, send = weight_sums(
        pair_in, plan, cot_parts, pre_act, ghosts, 0, factor, tile_count, 2
    )
    got_two = trade(send, 0)
    far, near, sent = tie(far, near, send)
    pre_parts = (grad_pre, near, far, swap_part(far, 1))
    keep_one, across_one, across_zero, across_both = weight_sums(
        pair_in, plan, pre_parts, features, ghosts, 1, factor, tile_count, 4
    )
    got_two, across_one = tie(got_two, across_one)
    got_zero, got_both = trade(across_zero, 0), trade(across_both, 0, 1)
    keep_two, send = merge(keep_two, got_two, across_one)
    got_one = trade(send, 1)
    pre_parts, keep_one = tie(pre_parts, keep_one)
    local_one, backs = partial_sums(pair_in, plan, pre_parts, weight_one, slot_count)
    got_one, backs = tie(got_one, backs)
    shares = [[0, 1], [2], list(range(3, len(backs)))]
    returned = [None] * len(backs)

    def beside(value, step):
        share = shares.pop(0) if shares else []
        value, mine = tie(value, [backs[g] for g in share])
        got, landed = tie(trade(value, step), give(mine, [back_lists[g] for g in share]))
        for group, back in zip(share, landed):
            returned[group] = back
        return got

    arrived = (keep_two, got_one, keep_one, got_zero, got_both)
    sources = (((0, None), (1, 0)), ((2, None), (1, 1), (3, None), (4, None)))
    for step in range(2, steps):
        keep, send = halve(step, sources, *arrived)
        got = beside(send, step)
        arrived, sources = (keep, got), tuple(((0, part), (1, part)) for part in range(2))
    chunk = (keep + got.astype(F32)).astype(BF16)[None]
    for step in reversed(range(2, steps)):
        got = beside(chunk, step)
        chunk = jnp.concatenate([chunk, got], axis=0)
    share = sum(shares, [])
    chunk, mine = tie(chunk, [backs[g] for g in share])
    quarters = (chunk, trade(chunk, 1), trade(chunk, 0), trade(chunk, 0, 1))
    for group, back in zip(share, give(mine, [back_lists[g] for g in share])):
        returned[group] = back
    grad_features = settle(False, send_list, plan, local_one, cotangent, returned)
    sum_two, sum_one = unpack(quarters, rows, columns)
    shape = (offset_count, width, columns)
    return grad_features, sum_one.reshape(shape), sum_two.reshape(shape)


def solution(mesh):
    return jax.shard_map(
        shards,
        mesh=mesh,
        in_specs=(
            P("chan", "tile"),
            P("chan", "tile"),
            P("chan", "tile"),
            P(None, "chan", None),
            P(None, "chan", None),
            P("tile", None, None),
            P("tile", None, None),
            P("tile", None, None),
        ),
        out_specs=(P("chan", "tile"), P(None, "chan", None), P(None, "chan", None)),
        check_vma=False,
    )
```

```python
import functools
import math

import jax
import jax.numpy as jnp
import numpy as np
from jax import lax
from jax.experimental import pallas as pl
from jax.experimental.pallas import tpu as pltpu
from jax.sharding import PartitionSpec as P

TILE_Y = 4
STEP_ROW = (-1, -1, -1, 0, 0, 1, 1, 1)
STEP_COL = (-1, 0, 1, -1, 1, -1, 0, 1)

VMEM = pltpu.VMEM
SMEM = pltpu.SMEM
BF16 = jnp.bfloat16
F32 = jnp.float32


def call(kernel, name, outs, spaces, args, scratch=(), flops=0, vmem_mib=4, out_space="V"):
    memory = {"S": SMEM, "H": pltpu.HBM, "V": VMEM}
    spaces = spaces + "V" * (len(args) - len(spaces))
    moved = sum(a.size * a.dtype.itemsize for a in args)
    moved += sum(o.size * o.dtype.itemsize for o in outs)
    return pl.pallas_call(
        kernel,
        out_shape=list(outs),
        in_specs=[pl.BlockSpec(memory_space=memory[space]) for space in spaces],
        out_specs=[pl.BlockSpec(memory_space=memory[out_space])] * len(outs),
        scratch_shapes=list(scratch),
        name=name,
        cost_estimate=pl.CostEstimate(flops=flops, bytes_accessed=moved, transcendentals=0),
        compiler_params=pltpu.CompilerParams(vmem_limit_bytes=vmem_mib << 20),
    )(*(keep_in_hbm(a) if space == "H" else a for a, space in zip(args, spaces)))


def keep_in_hbm(value):
    return pltpu.with_memory_space_constraint(value, pltpu.HBM)


def struct(shape, dtype):
    return jax.ShapeDtypeStruct(shape, dtype)


def ghost_plan(tile_count, block_count, slot_count):
    rows = tile_count // TILE_Y

    def pairs_of(direction, keep=lambda tile: True):
        found = []
        for tile in range(tile_count):
            row = tile // TILE_Y + STEP_ROW[direction]
            col = tile % TILE_Y + STEP_COL[direction]
            if 0 <= row < rows and 0 <= col < TILE_Y and keep(tile):
                found.append((tile, row * TILE_Y + col, direction))
        return found

    groups = [
        pairs_of(4, lambda t: t % 2 == 1) + pairs_of(3, lambda t: t % 2 == 0),
        pairs_of(4, lambda t: t % 2 == 0) + pairs_of(3, lambda t: t % 2 == 1),
    ]
    for direction in (0, 7, 1, 6, 2, 5):
        pairs = pairs_of(direction)
        for group in groups[2:]:
            sources = {p[0] for p in group}
            targets = {p[1] for p in group}
            if all(p[0] not in sources and p[1] not in targets for p in pairs):
                group.extend(pairs)
                break
        else:
            groups.append(pairs)
    groups = [g for g in groups if g]
    trash = block_count + 8 * slot_count + 1
    plan = np.zeros((len(groups), 2, tile_count), np.int32)
    plan[:, 1] = trash
    for index, group in enumerate(groups):
        for source, target, direction in group:
            plan[index, 0, source] = direction
            plan[index, 1, target] = block_count + (7 - direction) * slot_count
    return [[(s, t) for s, t, _ in g] for g in groups], plan


def here(values):
    me = lax.axis_index("tile")
    common = int(np.bincount(values).argmax())
    found = jnp.int32(common)
    for tile, value in enumerate(values):
        if value != common:
            found = jnp.where(me == tile, jnp.int32(int(value)), found)
    return found


def pack_kernel(plan, lists_ref, *refs):
    count = plan.shape[0]
    sources, refs = refs[:4], refs[4:]
    out_refs, copied, sems = refs[:count], refs[count:-1], refs[-1]
    copies = [
        pltpu.make_async_copy(source, target, sems.at[index])
        for index, (source, target) in enumerate(zip(sources, copied))
    ]
    for copy in copies:
        copy.start()
    pre_ref, feat_ref = copied[:2]
    copies[0].wait()
    copies[1].wait()
    last = pre_ref.shape[1] // 128 - 1
    for index, out_ref in enumerate(out_refs):
        direction = here(plan[index, 0])
        for slot in range(out_ref.shape[1]):
            block = jnp.minimum(lists_ref[0, direction, slot], last)
            lanes = pl.ds(pl.multiple_of(block * 128, 128), 128)
            out_ref[0, slot] = jnp.maximum(pre_ref[:, lanes], 0)
            out_ref[1, slot] = feat_ref[:, lanes]
    copies[2].wait()
    copies[3].wait()


def pack(lists, plan, *sources):
    shape = struct((2, lists.shape[2], sources[0].shape[0], 128), BF16)
    result = call(
        functools.partial(pack_kernel, plan),
        "pack_sends",
        [shape] * plan.shape[0] + [struct(s.shape, s.dtype) for s in sources],
        "SHHHH",
        (lists, *sources),
        [pltpu.SemaphoreType.DMA((4,))],
    )
    return result[: plan.shape[0]], result[plan.shape[0] :]


def gather_full(parts, full):
    me = lax.axis_index("chan")
    width = parts[0].shape[0]
    for step, part in enumerate(parts):
        full[pl.ds(pl.multiple_of((me ^ step) * width, 16), width), :] = part[...]


def partial_kernel(plan, riders, pin_ref, weight_ref, *refs):
    group_count = plan.shape[0]
    parts, refs = refs[:4], refs[4:]
    ride_refs, refs = refs[: len(riders)], refs[len(riders) :]
    local_ref = refs[0]
    back_refs = refs[1 : 1 + group_count]
    full, even_product, odd_product, even, odd = refs[1 + group_count :]
    offset_count, block_count = pin_ref.shape[1:]
    width = local_ref.shape[1]
    gather_full(parts, full)
    even[...] = jnp.zeros_like(even)
    odd[...] = jnp.zeros_like(odd)

    def multiply(turn, product):
        lanes = pl.ds(pl.multiple_of(turn * 256, 256), 256)
        product[...] = jnp.dot(weight_ref[...], full[:, lanes], preferred_element_type=F32)

    def land(turn, product):
        for offset in range(offset_count):
            for half, total in enumerate((even, odd)):
                entry = pin_ref[0, offset, turn * 2 + half]
                total[entry] += product[
                    offset * width : (offset + 1) * width, half * 128 : (half + 1) * 128
                ]

    turns = block_count // 2
    multiply(0, even_product)

    def two_turns(step, _):
        multiply(2 * step + 1, odd_product)
        land(2 * step, even_product)
        multiply(jnp.minimum(2 * step + 2, turns - 1), even_product)
        land(2 * step + 1, odd_product)
        return 0

    lax.fori_loop(0, turns // 2, two_turns, 0)
    local_ref[...] = even[:block_count] + odd[:block_count]
    for index, back_ref in enumerate(back_refs):
        base = here(plan[index, 1])
        for slot in range(back_ref.shape[1]):
            back_ref[0, slot] = (even[base + slot] + odd[base + slot]).astype(BF16)
    for index, ride_ref in zip(riders, ride_refs):
        back_refs[index][1:] = ride_ref[...]


def partial_sums(pin, plan, parts, weight, slot_count, riders=(), rides=()):
    width, voxels = parts[0].shape
    offset_count, block_count = pin.shape[1:]
    entries = block_count + 9 * slot_count + 1
    outs = [struct((block_count, width, 128), F32)]
    for group in range(plan.shape[0]):
        outs.append(struct((3 if group in riders else 1, slot_count, width, 128), BF16))
    flat = weight.reshape(offset_count * width, 4 * width)
    result = call(
        functools.partial(partial_kernel, plan, riders),
        "partial_sums",
        outs,
        "S",
        (pin, flat, *parts, *rides),
        [
            VMEM((4 * width, voxels), BF16),
            VMEM((offset_count * width, 256), F32),
            VMEM((offset_count * width, 256), F32),
            VMEM((entries, width, 128), F32),
            VMEM((entries, width, 128), F32),
        ],
        flops=2 * weight.size * voxels,
        vmem_mib=12,
    )
    return result[0], result[1:]


def packed_rows(rows, tile_count):
    step = 16 * tile_count
    return -(-(rows + rows // 2) // step) * step


def weight_kernel(plan, which, factor, pieces, pin_ref, own_ref, *refs):
    parts, refs = refs[:4], refs[4:]
    ghost_refs, refs = refs[: plan.shape[0]], refs[plan.shape[0] :]
    piece_refs, refs = refs[:pieces], refs[pieces:]
    full, extended, gathered, wide, tall = refs
    offset_count, block_count = pin_ref.shape[1:]
    width = own_ref.shape[0]
    gather_full(parts, full)
    for block in range(block_count):
        value = own_ref[:, block * 128 : (block + 1) * 128]
        extended[block] = jnp.maximum(value, 0) if which == 0 else value
    for index, ghost_ref in enumerate(ghost_refs):
        base = here(plan[index, 1])
        for slot in range(ghost_ref.shape[1]):
            extended[base + slot] = ghost_ref[ghost_ref.shape[0] - 2 + which, slot]
    empty = block_count + 8 * ghost_refs[0].shape[1]
    extended[empty] = jnp.zeros_like(extended[empty])
    chunk = gathered.shape[0] // width

    def some_offsets(turn, _):
        for step in range(chunk):
            for block in range(block_count):
                entry = pin_ref[0, turn * chunk + step, block]
                gathered[step * width : (step + 1) * width, block * 128 : (block + 1) * 128] = (
                    extended[entry]
                )
        grads = lax.dot_general(
            gathered[...], full[...], (((1,), (1,)), ((), ())), preferred_element_type=F32
        )
        rows = chunk * width
        wide[pl.ds(pl.multiple_of(turn * rows, 16), rows), : grads.shape[1]] = grads * factor
        return 0

    lax.fori_loop(0, offset_count // chunk, some_offsets, 0)
    rows, half = wide.shape[0], wide.shape[0] // 2
    tall[:rows] = wide[:, :128]
    tall[rows : rows + half, :64] = wide[:half, 128:192]
    tall[rows : rows + half, 64:] = wide[half:, 128:192]
    if tall.shape[0] > rows + half:
        tall[rows + half :] = jnp.zeros((tall.shape[0] - rows - half, 128), F32)
    split = tall.shape[0] // pieces
    mine = exchange_bit(0) if pieces == 2 else 2 * exchange_bit(0) + exchange_bit(1)
    for index, piece_ref in enumerate(piece_refs):
        piece = tall[pl.ds(pl.multiple_of((mine ^ index) * split, 16), split), :]
        piece_ref[...] = piece.astype(piece_ref.dtype)


def weight_sums(pin, plan, parts, own, ghosts, which, factor, tile_count, pieces):
    width, voxels = own.shape
    offset_count, block_count = pin.shape[1:]
    slot_count = ghosts[0].shape[1]
    entries = block_count + 9 * slot_count + 1
    chunk = 9 if offset_count % 9 == 0 else 1
    rows = offset_count * width
    tall = packed_rows(rows, tile_count)
    shape = (tall // pieces, 128)
    return call(
        functools.partial(weight_kernel, plan, which, factor, pieces),
        "weight_sums",
        [struct(shape, F32)] + [struct(shape, BF16)] * (pieces - 1),
        "S",
        (pin, own, *parts, *ghosts),
        [
            VMEM((4 * width, voxels), BF16),
            VMEM((entries, width, 128), BF16),
            VMEM((chunk * width, voxels), BF16),
            VMEM((rows, 256), F32),
            VMEM((tall, 128), F32),
        ],
        flops=2 * rows * 4 * width * voxels,
        vmem_mib=14,
    )


def settle_kernel(plan, first, lists_ref, other_ref, local_ref, *refs):
    *back_refs, out_ref, total = refs
    block_count = local_ref.shape[0]
    total[:block_count] = local_ref[...]
    for index, back_ref in enumerate(back_refs):
        direction = here(plan[index, 0])
        for slot in range(back_ref.shape[1]):
            block = lists_ref[0, direction, slot]
            total[block] += back_ref[0, slot].astype(F32)
    for block in range(block_count):
        lanes = slice(block * 128, (block + 1) * 128)
        other = other_ref[:, lanes].astype(F32)
        if first:
            value = jnp.where(other > 0, total[block], 0.0)
        else:
            value = other + total[block]
        out_ref[:, lanes] = value.astype(BF16)


def settle(first, lists, plan, local, other, backs):
    block_count, width, _ = local.shape
    return call(
        functools.partial(settle_kernel, plan, first),
        "settle",
        [struct(other.shape, BF16)],
        "S",
        (lists, other, local, *backs),
        [VMEM((block_count + 1, width, 128), F32)],
        flops=local.size,
    )[0]


def exchange_dim(step):
    parity = lax.axis_index("chan") % 2
    if step < 2:
        return jnp.where(parity == 0, step, 1 - step)
    return step


def exchange_bit(step):
    return lax.shift_right_logical(lax.axis_index("tile"), exchange_dim(step)) & 1


def trade(value, *steps):
    tile_count = lax.axis_size("tile")
    chan_count = lax.axis_size("chan")
    pairs = []
    for tile in range(tile_count):
        for chan in range(chan_count):
            dims = [(1 - step if chan % 2 else step) if step < 2 else step for step in steps]
            other = tile ^ sum(1 << dim for dim in dims)
            pairs.append((tile * chan_count + chan, other * chan_count + chan))
    return lax.ppermute(value, ("tile", "chan"), pairs)


def halve_kernel(step, sources, *refs):
    *_, next_ref, send_ref = refs
    bit = exchange_bit(step)
    split = next_ref.shape[1]
    mine = pl.ds(pl.multiple_of(bit * split, 16), split)
    theirs = pl.ds(pl.multiple_of((1 - bit) * split, 16), split)
    for index, terms in enumerate(sources):
        views = [refs[term] if part is None else refs[term].at[part] for term, part in terms]
        next_ref[index] = sum(view[mine, :].astype(F32) for view in views)
        send_ref[index] = sum(view[theirs, :].astype(F32) for view in views).astype(BF16)


def halve(step, sources, *args):
    shape = (len(sources), args[0].shape[-2] // 2, 128)
    return call(
        functools.partial(halve_kernel, step, sources),
        "halve",
        [struct(shape, F32), struct(shape, BF16)],
        "",
        args,
        flops=2 * args[0].size,
    )


def merge_kernel(keep_ref, got_ref, other_ref, next_ref, send_ref):
    bit = exchange_bit(1)
    split = next_ref.shape[0]
    mine = pl.ds(pl.multiple_of(bit * split, 16), split)
    theirs = pl.ds(pl.multiple_of((1 - bit) * split, 16), split)
    next_ref[...] = keep_ref[mine, :] + got_ref[mine, :].astype(F32)
    send_ref[0] = (keep_ref[theirs, :] + got_ref[theirs, :].astype(F32)).astype(BF16)
    send_ref[1] = other_ref[...]


def merge(keep, got, other):
    return call(
        merge_kernel,
        "merge_sends",
        [struct(other.shape, F32), struct((2,) + other.shape, BF16)],
        "",
        (keep, got, other),
        flops=keep.size,
    )


def unpack_kernel(tile_count, *refs):
    quarters, out_hbm, (wide, tall, sems) = refs[:4], refs[4:6], refs[6:]
    steps = tile_count.bit_length() - 1
    count, _, chunk, _ = quarters[0].shape
    rows = wide.shape[1]
    half = rows // 2
    mine = 0
    for step in range(steps):
        mine = mine * 2 + exchange_bit(step)
    copies = []
    for part in range(2):
        for index in range(tile_count):
            place = pl.ds(pl.multiple_of((mine ^ index) * chunk, 16), chunk)
            tall[place, :] = quarters[index // count][index % count, part].astype(F32)
        for side in range(2):
            here_rows = slice(side * half, (side + 1) * half)
            wide[part, here_rows, :128] = tall[here_rows]
            wide[part, here_rows, 128:192] = tall[rows : rows + half, side * 64 : side * 64 + 64]
            copies.append(
                pltpu.make_async_copy(
                    wide.at[part, here_rows],
                    out_hbm[part].at[here_rows],
                    sems.at[2 * part + side],
                )
            )
            copies[-1].start()
    for copy in copies:
        copy.wait()


def unpack(quarters, rows, columns):
    tile_count = 4 * quarters[0].shape[0]
    return call(
        functools.partial(unpack_kernel, tile_count),
        "unpack_sums",
        [struct((rows, columns), F32)] * 2,
        "",
        quarters,
        [
            VMEM((2, rows, columns), F32),
            VMEM((tile_count * quarters[0].shape[2], 128), F32),
            pltpu.SemaphoreType.DMA((4,)),
        ],
        vmem_mib=8,
        out_space="H",
    )


def swap_part(value, bits):
    return lax.ppermute(value, "chan", [(i, i ^ bits) for i in range(4)])


def shards(features, pre_act, cotangent, weight_one, weight_two, send_list, pair_in, pair_out):
    tile_count = lax.axis_size("tile")
    width, voxels = features.shape
    offset_count, _, columns = weight_one.shape
    block_count = pair_out.shape[2]
    slot_count = send_list.shape[2]
    rows = offset_count * width
    steps = tile_count.bit_length() - 1
    pair_lists, plan = ghost_plan(tile_count, block_count, slot_count)
    factor = 1.0 / math.sqrt(tile_count * voxels)
    tie = lambda *values: lax.optimization_barrier(values)

    def give(values, lists):
        return [lax.ppermute(v, "tile", p) for v, p in zip(values, lists)]

    back_lists = [[(t, s) for s, t in p] for p in pair_lists]

    early = range(2, min(4, len(pair_lists)))
    riders = [g for g in range(len(pair_lists)) if g not in early]

    far, near, last = (swap_part(cotangent, bits) for bits in (2, 1, 3))
    sends, here_now = pack(send_list, plan, pre_act, features, cotangent, weight_two)
    pre_act, features, cotangent, weight_two = here_now
    soon = give([sends[g] for g in early], [pair_lists[g] for g in early])
    cot_parts = (cotangent, near, far, last)
    local_two, backs = partial_sums(
        pair_in, plan, cot_parts, weight_two, slot_count, riders, [sends[g] for g in riders]
    )
    backs, soon = tie(give(backs, back_lists), soon)
    grad_pre = settle(True, send_list, plan, local_two, pre_act, backs)

    ghosts = list(backs)
    for group, ghost in zip(early, soon):
        ghosts[group] = ghost
    far, near = swap_part(grad_pre, 2), swap_part(grad_pre, 1)
    keep_two, send = weight_sums(
        pair_in, plan, cot_parts, pre_act, ghosts, 0, factor, tile_count, 2
    )
    got_two = trade(send, 0)
    far, near, sent = tie(far, near, send)
    pre_parts = (grad_pre, near, far, swap_part(far, 1))
    keep_one, across_one, across_zero, across_both = weight_sums(
        pair_in, plan, pre_parts, features, ghosts, 1, factor, tile_count, 4
    )
    got_two, across_one = tie(got_two, across_one)
    got_zero, got_both = trade(across_zero, 0), trade(across_both, 0, 1)
    keep_two, send = merge(keep_two, got_two, across_one)
    got_one = trade(send, 1)
    pre_parts, keep_one = tie(pre_parts, keep_one)
    local_one, backs = partial_sums(pair_in, plan, pre_parts, weight_one, slot_count)
    got_one, backs = tie(got_one, backs)
    shares = [[0, 1], [3], [2] + list(range(4, len(backs)))]
    returned = [None] * len(backs)

    def beside(value, step):
        share = shares.pop(0) if shares else []
        value, mine = tie(value, [backs[g] for g in share])
        got, landed = tie(trade(value, step), give(mine, [back_lists[g] for g in share]))
        for group, back in zip(share, landed):
            returned[group] = back
        return got

    arrived = (keep_two, got_one, keep_one, got_zero, got_both)
    sources = (((0, None), (1, 0)), ((2, None), (1, 1), (3, None), (4, None)))
    for step in range(2, steps):
        keep, send = halve(step, sources, *arrived)
        got = beside(send, step)
        arrived, sources = (keep, got), tuple(((0, part), (1, part)) for part in range(2))
    chunk = (keep + got.astype(F32)).astype(BF16)[None]
    for step in reversed(range(2, steps)):
        got = beside(chunk, step)
        chunk = jnp.concatenate([chunk, got], axis=0)
    share = sum(shares, [])
    chunk, mine = tie(chunk, [backs[g] for g in share])
    quarters = (chunk, trade(chunk, 1), trade(chunk, 0), trade(chunk, 0, 1))
    for group, back in zip(share, give(mine, [back_lists[g] for g in share])):
        returned[group] = back
    grad_features = settle(False, send_list, plan, local_one, cotangent, returned)
    sum_two, sum_one = unpack(quarters, rows, columns)
    shape = (offset_count, width, columns)
    return grad_features, sum_one.reshape(shape), sum_two.reshape(shape)


def solution(mesh):
    return jax.shard_map(
        shards,
        mesh=mesh,
        in_specs=(
            P("chan", "tile"),
            P("chan", "tile"),
            P("chan", "tile"),
            P(None, "chan", None),
            P(None, "chan", None),
            P("tile", None, None),
            P("tile", None, None),
            P("tile", None, None),
        ),
        out_specs=(P("chan", "tile"), P(None, "chan", None), P(None, "chan", None)),
        check_vma=False,
    )
```

```python
import functools
import math

import jax
import jax.numpy as jnp
import numpy as np
from jax import lax
from jax.experimental import pallas as pl
from jax.experimental.pallas import tpu as pltpu
from jax.sharding import PartitionSpec as P

TILE_Y = 4
STEP_ROW = (-1, -1, -1, 0, 0, 1, 1, 1)
STEP_COL = (-1, 0, 1, -1, 1, -1, 0, 1)

VMEM = pltpu.VMEM
SMEM = pltpu.SMEM
BF16 = jnp.bfloat16
F32 = jnp.float32


def call(kernel, name, outs, spaces, args, scratch=(), flops=0, vmem_mib=4, out_space="V"):
    memory = {"S": SMEM, "H": pltpu.HBM, "V": VMEM}
    spaces = spaces + "V" * (len(args) - len(spaces))
    moved = sum(a.size * a.dtype.itemsize for a in args)
    moved += sum(o.size * o.dtype.itemsize for o in outs)
    return pl.pallas_call(
        kernel,
        out_shape=list(outs),
        in_specs=[pl.BlockSpec(memory_space=memory[space]) for space in spaces],
        out_specs=[pl.BlockSpec(memory_space=memory[out_space])] * len(outs),
        scratch_shapes=list(scratch),
        name=name,
        cost_estimate=pl.CostEstimate(flops=flops, bytes_accessed=moved, transcendentals=0),
        compiler_params=pltpu.CompilerParams(vmem_limit_bytes=vmem_mib << 20),
    )(*(keep_in_hbm(a) if space == "H" else a for a, space in zip(args, spaces)))


def keep_in_hbm(value):
    return pltpu.with_memory_space_constraint(value, pltpu.HBM)


def struct(shape, dtype):
    return jax.ShapeDtypeStruct(shape, dtype)


def ghost_plan(tile_count, block_count, slot_count):
    rows = tile_count // TILE_Y

    def pairs_of(direction, keep=lambda tile: True):
        found = []
        for tile in range(tile_count):
            row = tile // TILE_Y + STEP_ROW[direction]
            col = tile % TILE_Y + STEP_COL[direction]
            if 0 <= row < rows and 0 <= col < TILE_Y and keep(tile):
                found.append((tile, row * TILE_Y + col, direction))
        return found

    groups = [
        pairs_of(4, lambda t: t % 2 == 1) + pairs_of(3, lambda t: t % 2 == 0),
        pairs_of(4, lambda t: t % 2 == 0) + pairs_of(3, lambda t: t % 2 == 1),
    ]
    for direction in (0, 7, 1, 6, 2, 5):
        pairs = pairs_of(direction)
        for group in groups[2:]:
            sources = {p[0] for p in group}
            targets = {p[1] for p in group}
            if all(p[0] not in sources and p[1] not in targets for p in pairs):
                group.extend(pairs)
                break
        else:
            groups.append(pairs)
    groups = [g for g in groups if g]
    trash = block_count + 8 * slot_count + 1
    plan = np.zeros((len(groups), 2, tile_count), np.int32)
    plan[:, 1] = trash
    for index, group in enumerate(groups):
        for source, target, direction in group:
            plan[index, 0, source] = direction
            plan[index, 1, target] = block_count + (7 - direction) * slot_count
    return [[(s, t) for s, t, _ in g] for g in groups], plan


def here(values):
    me = lax.axis_index("tile")
    common = int(np.bincount(values).argmax())
    found = jnp.int32(common)
    for tile, value in enumerate(values):
        if value != common:
            found = jnp.where(me == tile, jnp.int32(int(value)), found)
    return found


def pack_kernel(plan, lists_ref, *refs):
    count = plan.shape[0]
    sources, refs = refs[:4], refs[4:]
    out_refs, copied, sems = refs[:count], refs[count:-1], refs[-1]
    copies = [
        pltpu.make_async_copy(source, target, sems.at[index])
        for index, (source, target) in enumerate(zip(sources, copied))
    ]
    for copy in copies:
        copy.start()
    pre_ref, feat_ref = copied[:2]
    copies[0].wait()
    copies[1].wait()
    last = pre_ref.shape[1] // 128 - 1
    for index, out_ref in enumerate(out_refs):
        direction = here(plan[index, 0])
        for slot in range(out_ref.shape[1]):
            block = jnp.minimum(lists_ref[0, direction, slot], last)
            lanes = pl.ds(pl.multiple_of(block * 128, 128), 128)
            out_ref[0, slot] = jnp.maximum(pre_ref[:, lanes], 0)
            out_ref[1, slot] = feat_ref[:, lanes]
    copies[2].wait()
    copies[3].wait()


def pack(lists, plan, *sources):
    shape = struct((2, lists.shape[2], sources[0].shape[0], 128), BF16)
    result = call(
        functools.partial(pack_kernel, plan),
        "pack_sends",
        [shape] * plan.shape[0] + [struct(s.shape, s.dtype) for s in sources],
        "SHHHH",
        (lists, *sources),
        [pltpu.SemaphoreType.DMA((4,))],
    )
    return result[: plan.shape[0]], result[plan.shape[0] :]


def gather_full(parts, full):
    me = lax.axis_index("chan")
    width = parts[0].shape[0]
    for step, part in enumerate(parts):
        full[pl.ds(pl.multiple_of((me ^ step) * width, 16), width), :] = part[...]


def partial_kernel(plan, riders, pin_ref, weight_ref, *refs):
    group_count = plan.shape[0]
    parts, refs = refs[:4], refs[4:]
    ride_refs, refs = refs[: len(riders)], refs[len(riders) :]
    local_ref = refs[0]
    back_refs = refs[1 : 1 + group_count]
    full, even_product, odd_product, even, odd = refs[1 + group_count :]
    offset_count, block_count = pin_ref.shape[1:]
    width = local_ref.shape[1]
    gather_full(parts, full)
    even[...] = jnp.zeros_like(even)
    odd[...] = jnp.zeros_like(odd)

    def multiply(turn, product):
        lanes = pl.ds(pl.multiple_of(turn * 256, 256), 256)
        product[...] = jnp.dot(weight_ref[...], full[:, lanes], preferred_element_type=F32)

    def land(turn, product):
        for offset in range(offset_count):
            for half, total in enumerate((even, odd)):
                entry = pin_ref[0, offset, turn * 2 + half]
                total[entry] += product[
                    offset * width : (offset + 1) * width, half * 128 : (half + 1) * 128
                ]

    turns = block_count // 2
    multiply(0, even_product)

    def two_turns(step, _):
        multiply(2 * step + 1, odd_product)
        land(2 * step, even_product)
        multiply(jnp.minimum(2 * step + 2, turns - 1), even_product)
        land(2 * step + 1, odd_product)
        return 0

    lax.fori_loop(0, turns // 2, two_turns, 0)
    local_ref[...] = even[:block_count] + odd[:block_count]
    for index, back_ref in enumerate(back_refs):
        base = here(plan[index, 1])
        for slot in range(back_ref.shape[1]):
            back_ref[0, slot] = (even[base + slot] + odd[base + slot]).astype(BF16)
    for index, ride_ref in zip(riders, ride_refs):
        back_refs[index][1:] = ride_ref[...]


def partial_sums(pin, plan, parts, weight, slot_count, riders=(), rides=()):
    width, voxels = parts[0].shape
    offset_count, block_count = pin.shape[1:]
    entries = block_count + 9 * slot_count + 1
    outs = [struct((block_count, width, 128), F32)]
    for group in range(plan.shape[0]):
        outs.append(struct((3 if group in riders else 1, slot_count, width, 128), BF16))
    flat = weight.reshape(offset_count * width, 4 * width)
    result = call(
        functools.partial(partial_kernel, plan, riders),
        "partial_sums",
        outs,
        "S",
        (pin, flat, *parts, *rides),
        [
            VMEM((4 * width, voxels), BF16),
            VMEM((offset_count * width, 256), F32),
            VMEM((offset_count * width, 256), F32),
            VMEM((entries, width, 128), F32),
            VMEM((entries, width, 128), F32),
        ],
        flops=2 * weight.size * voxels,
        vmem_mib=12,
    )
    return result[0], result[1:]


def packed_rows(rows, tile_count):
    step = 8 * tile_count
    return -(-(rows + rows // 2) // step) * step


def weight_kernel(plan, which, factor, pieces, pin_ref, own_ref, *refs):
    parts, refs = refs[:4], refs[4:]
    ghost_refs, refs = refs[: plan.shape[0]], refs[plan.shape[0] :]
    piece_refs, refs = refs[:pieces], refs[pieces:]
    full, extended, gathered, wide, tall = refs
    offset_count, block_count = pin_ref.shape[1:]
    width = own_ref.shape[0]
    gather_full(parts, full)
    for block in range(block_count):
        value = own_ref[:, block * 128 : (block + 1) * 128]
        extended[block] = jnp.maximum(value, 0) if which == 0 else value
    for index, ghost_ref in enumerate(ghost_refs):
        base = here(plan[index, 1])
        for slot in range(ghost_ref.shape[1]):
            extended[base + slot] = ghost_ref[ghost_ref.shape[0] - 2 + which, slot]
    empty = block_count + 8 * ghost_refs[0].shape[1]
    extended[empty] = jnp.zeros_like(extended[empty])
    chunk = gathered.shape[0] // width

    def some_offsets(turn, _):
        for step in range(chunk):
            for block in range(block_count):
                entry = pin_ref[0, turn * chunk + step, block]
                gathered[step * width : (step + 1) * width, block * 128 : (block + 1) * 128] = (
                    extended[entry]
                )
        grads = lax.dot_general(
            gathered[...], full[...], (((1,), (1,)), ((), ())), preferred_element_type=F32
        )
        rows = chunk * width
        wide[pl.ds(pl.multiple_of(turn * rows, 16), rows), : grads.shape[1]] = grads * factor
        return 0

    lax.fori_loop(0, offset_count // chunk, some_offsets, 0)
    rows, half = wide.shape[0], wide.shape[0] // 2
    tall[:rows] = wide[:, :128]
    tall[rows : rows + half, :64] = wide[:half, 128:192]
    tall[rows : rows + half, 64:] = wide[half:, 128:192]
    if tall.shape[0] > rows + half:
        tall[rows + half :] = jnp.zeros((tall.shape[0] - rows - half, 128), F32)
    split = tall.shape[0] // pieces
    mine = exchange_bit(0) if pieces == 2 else 2 * exchange_bit(0) + exchange_bit(1)
    for index, piece_ref in enumerate(piece_refs):
        piece = tall[pl.ds(pl.multiple_of((mine ^ index) * split, 8), split), :]
        piece_ref[...] = piece.astype(piece_ref.dtype)


def weight_sums(pin, plan, parts, own, ghosts, which, factor, tile_count, pieces):
    width, voxels = own.shape
    offset_count, block_count = pin.shape[1:]
    slot_count = ghosts[0].shape[1]
    entries = block_count + 9 * slot_count + 1
    chunk = 9 if offset_count % 9 == 0 else 1
    rows = offset_count * width
    tall = packed_rows(rows, tile_count)
    shape = (tall // pieces, 128)
    return call(
        functools.partial(weight_kernel, plan, which, factor, pieces),
        "weight_sums",
        [struct(shape, F32)] + [struct(shape, BF16)] * (pieces - 1),
        "S",
        (pin, own, *parts, *ghosts),
        [
            VMEM((4 * width, voxels), BF16),
            VMEM((entries, width, 128), BF16),
            VMEM((chunk * width, voxels), BF16),
            VMEM((rows, 256), F32),
            VMEM((tall, 128), F32),
        ],
        flops=2 * rows * 4 * width * voxels,
        vmem_mib=14,
    )


def settle_kernel(plan, first, lists_ref, other_ref, local_ref, *refs):
    *back_refs, out_ref, total = refs
    block_count = local_ref.shape[0]
    total[:block_count] = local_ref[...]
    for index, back_ref in enumerate(back_refs):
        direction = here(plan[index, 0])
        for slot in range(back_ref.shape[1]):
            block = lists_ref[0, direction, slot]
            total[block] += back_ref[0, slot].astype(F32)
    for block in range(block_count):
        lanes = slice(block * 128, (block + 1) * 128)
        other = other_ref[:, lanes].astype(F32)
        if first:
            value = jnp.where(other > 0, total[block], 0.0)
        else:
            value = other + total[block]
        out_ref[:, lanes] = value.astype(BF16)


def settle(first, lists, plan, local, other, backs):
    block_count, width, _ = local.shape
    return call(
        functools.partial(settle_kernel, plan, first),
        "settle",
        [struct(other.shape, BF16)],
        "S",
        (lists, other, local, *backs),
        [VMEM((block_count + 1, width, 128), F32)],
        flops=local.size,
    )[0]


def exchange_dim(step):
    parity = lax.axis_index("chan") % 2
    if step < 2:
        return jnp.where(parity == 0, step, 1 - step)
    return step


def exchange_bit(step):
    return lax.shift_right_logical(lax.axis_index("tile"), exchange_dim(step)) & 1


def trade(value, *steps):
    tile_count = lax.axis_size("tile")
    chan_count = lax.axis_size("chan")
    pairs = []
    for tile in range(tile_count):
        for chan in range(chan_count):
            dims = [(1 - step if chan % 2 else step) if step < 2 else step for step in steps]
            other = tile ^ sum(1 << dim for dim in dims)
            pairs.append((tile * chan_count + chan, other * chan_count + chan))
    return lax.ppermute(value, ("tile", "chan"), pairs)


def halve_kernel(step, sources, *refs):
    *_, next_ref, send_ref = refs
    bit = exchange_bit(step)
    split = next_ref.shape[1]
    mine = pl.ds(pl.multiple_of(bit * split, 8), split)
    theirs = pl.ds(pl.multiple_of((1 - bit) * split, 8), split)
    for index, terms in enumerate(sources):
        views = [refs[term] if part is None else refs[term].at[part] for term, part in terms]
        next_ref[index] = sum(view[mine, :].astype(F32) for view in views)
        send_ref[index] = sum(view[theirs, :].astype(F32) for view in views).astype(BF16)


def halve(step, sources, *args):
    shape = (len(sources), args[0].shape[-2] // 2, 128)
    return call(
        functools.partial(halve_kernel, step, sources),
        "halve",
        [struct(shape, F32), struct(shape, BF16)],
        "",
        args,
        flops=2 * args[0].size,
    )


def merge_kernel(keep_ref, got_ref, other_ref, next_ref, send_ref):
    bit = exchange_bit(1)
    split = next_ref.shape[0]
    mine = pl.ds(pl.multiple_of(bit * split, 8), split)
    theirs = pl.ds(pl.multiple_of((1 - bit) * split, 8), split)
    next_ref[...] = keep_ref[mine, :] + got_ref[mine, :].astype(F32)
    send_ref[0] = (keep_ref[theirs, :] + got_ref[theirs, :].astype(F32)).astype(BF16)
    send_ref[1] = other_ref[...]


def merge(keep, got, other):
    return call(
        merge_kernel,
        "merge_sends",
        [struct(other.shape, F32), struct((2,) + other.shape, BF16)],
        "",
        (keep, got, other),
        flops=keep.size,
    )


def unpack_kernel(tile_count, *refs):
    quarters, out_hbm, (wide, tall, sems) = refs[:4], refs[4:6], refs[6:]
    steps = tile_count.bit_length() - 1
    count, _, chunk, _ = quarters[0].shape
    rows = wide.shape[1]
    half = rows // 2
    mine = 0
    for step in range(steps):
        mine = mine * 2 + exchange_bit(step)
    copies = []
    for part in range(2):
        for index in range(tile_count):
            place = pl.ds(pl.multiple_of((mine ^ index) * chunk, 8), chunk)
            tall[place, :] = quarters[index // count][index % count, part].astype(F32)
        for side in range(2):
            here_rows = slice(side * half, (side + 1) * half)
            wide[part, here_rows, :128] = tall[here_rows]
            wide[part, here_rows, 128:192] = tall[rows : rows + half, side * 64 : side * 64 + 64]
            copies.append(
                pltpu.make_async_copy(
                    wide.at[part, here_rows],
                    out_hbm[part].at[here_rows],
                    sems.at[2 * part + side],
                )
            )
            copies[-1].start()
    for copy in copies:
        copy.wait()


def unpack(quarters, rows, columns):
    tile_count = 4 * quarters[0].shape[0]
    return call(
        functools.partial(unpack_kernel, tile_count),
        "unpack_sums",
        [struct((rows, columns), F32)] * 2,
        "",
        quarters,
        [
            VMEM((2, rows, columns), F32),
            VMEM((tile_count * quarters[0].shape[2], 128), F32),
            pltpu.SemaphoreType.DMA((4,)),
        ],
        vmem_mib=8,
        out_space="H",
    )


def swap_part(value, bits):
    return lax.ppermute(value, "chan", [(i, i ^ bits) for i in range(4)])


def shards(features, pre_act, cotangent, weight_one, weight_two, send_list, pair_in, pair_out):
    tile_count = lax.axis_size("tile")
    width, voxels = features.shape
    offset_count, _, columns = weight_one.shape
    block_count = pair_out.shape[2]
    slot_count = send_list.shape[2]
    rows = offset_count * width
    steps = tile_count.bit_length() - 1
    pair_lists, plan = ghost_plan(tile_count, block_count, slot_count)
    factor = 1.0 / math.sqrt(tile_count * voxels)
    tie = lambda *values: lax.optimization_barrier(values)

    def give(values, lists):
        return [lax.ppermute(v, "tile", p) for v, p in zip(values, lists)]

    back_lists = [[(t, s) for s, t in p] for p in pair_lists]

    early = range(2, min(4, len(pair_lists)))
    riders = [g for g in range(len(pair_lists)) if g not in early]

    far, near, last = (swap_part(cotangent, bits) for bits in (2, 1, 3))
    sends, here_now = pack(send_list, plan, pre_act, features, cotangent, weight_two)
    pre_act, features, cotangent, weight_two = here_now
    soon = give([sends[g] for g in early], [pair_lists[g] for g in early])
    cot_parts = (cotangent, near, far, last)
    local_two, backs = partial_sums(
        pair_in, plan, cot_parts, weight_two, slot_count, riders, [sends[g] for g in riders]
    )
    backs, soon = tie(give(backs, back_lists), soon)
    grad_pre = settle(True, send_list, plan, local_two, pre_act, backs)

    ghosts = list(backs)
    for group, ghost in zip(early, soon):
        ghosts[group] = ghost
    far, near = swap_part(grad_pre, 2), swap_part(grad_pre, 1)
    keep_two, send = weight_sums(
        pair_in, plan, cot_parts, pre_act, ghosts, 0, factor, tile_count, 2
    )
    got_two = trade(send, 0)
    far, near, sent = tie(far, near, send)
    pre_parts = (grad_pre, near, far, swap_part(far, 1))
    keep_one, across_one, across_zero, across_both = weight_sums(
        pair_in, plan, pre_parts, features, ghosts, 1, factor, tile_count, 4
    )
    got_two, across_one = tie(got_two, across_one)
    got_zero, got_both = trade(across_zero, 0), trade(across_both, 0, 1)
    keep_two, send = merge(keep_two, got_two, across_one)
    got_one = trade(send, 1)
    pre_parts, keep_one = tie(pre_parts, keep_one)
    local_one, backs = partial_sums(pair_in, plan, pre_parts, weight_one, slot_count)
    got_one, backs = tie(got_one, backs)
    shares = [[0, 1], [3], [2] + list(range(4, len(backs)))]
    returned = [None] * len(backs)

    def beside(value, step):
        share = shares.pop(0) if shares else []
        value, mine = tie(value, [backs[g] for g in share])
        got, landed = tie(trade(value, step), give(mine, [back_lists[g] for g in share]))
        for group, back in zip(share, landed):
            returned[group] = back
        return got

    arrived = (keep_two, got_one, keep_one, got_zero, got_both)
    sources = (((0, None), (1, 0)), ((2, None), (1, 1), (3, None), (4, None)))
    for step in range(2, steps):
        keep, send = halve(step, sources, *arrived)
        got = beside(send, step)
        arrived, sources = (keep, got), tuple(((0, part), (1, part)) for part in range(2))
    chunk = (keep + got.astype(F32)).astype(BF16)[None]
    for step in reversed(range(2, steps)):
        got = beside(chunk, step)
        chunk = jnp.concatenate([chunk, got], axis=0)
    share = sum(shares, [])
    chunk, mine = tie(chunk, [backs[g] for g in share])
    quarters = (chunk, trade(chunk, 1), trade(chunk, 0), trade(chunk, 0, 1))
    for group, back in zip(share, give(mine, [back_lists[g] for g in share])):
        returned[group] = back
    grad_features = settle(False, send_list, plan, local_one, cotangent, returned)
    sum_two, sum_one = unpack(quarters, rows, columns)
    shape = (offset_count, width, columns)
    return grad_features, sum_one.reshape(shape), sum_two.reshape(shape)


def solution(mesh):
    return jax.shard_map(
        shards,
        mesh=mesh,
        in_specs=(
            P("chan", "tile"),
            P("chan", "tile"),
            P("chan", "tile"),
            P(None, "chan", None),
            P(None, "chan", None),
            P("tile", None, None),
            P("tile", None, None),
            P("tile", None, None),
        ),
        out_specs=(P("chan", "tile"), P(None, "chan", None), P(None, "chan", None)),
        check_vma=False,
    )
```

```python
import functools
import math

import jax
import jax.numpy as jnp
import numpy as np
from jax import lax
from jax.experimental import pallas as pl
from jax.experimental.pallas import tpu as pltpu
from jax.sharding import PartitionSpec as P

TILE_Y = 4
STEP_ROW = (-1, -1, -1, 0, 0, 1, 1, 1)
STEP_COL = (-1, 0, 1, -1, 1, -1, 0, 1)

VMEM = pltpu.VMEM
SMEM = pltpu.SMEM
BF16 = jnp.bfloat16
F32 = jnp.float32


def call(kernel, name, outs, spaces, args, scratch=(), flops=0, vmem_mib=4, out_space="V"):
    memory = {"S": SMEM, "H": pltpu.HBM, "V": VMEM}
    spaces = spaces + "V" * (len(args) - len(spaces))
    moved = sum(a.size * a.dtype.itemsize for a in args)
    moved += sum(o.size * o.dtype.itemsize for o in outs)
    return pl.pallas_call(
        kernel,
        out_shape=list(outs),
        in_specs=[pl.BlockSpec(memory_space=memory[space]) for space in spaces],
        out_specs=[pl.BlockSpec(memory_space=memory[out_space])] * len(outs),
        scratch_shapes=list(scratch),
        name=name,
        cost_estimate=pl.CostEstimate(flops=flops, bytes_accessed=moved, transcendentals=0),
        compiler_params=pltpu.CompilerParams(vmem_limit_bytes=vmem_mib << 20),
    )(*(keep_in_hbm(a) if space == "H" else a for a, space in zip(args, spaces)))


def keep_in_hbm(value):
    return pltpu.with_memory_space_constraint(value, pltpu.HBM)


def struct(shape, dtype):
    return jax.ShapeDtypeStruct(shape, dtype)


def ghost_plan(tile_count, block_count, slot_count):
    rows = tile_count // TILE_Y

    def pairs_of(direction, keep=lambda tile: True):
        found = []
        for tile in range(tile_count):
            row = tile // TILE_Y + STEP_ROW[direction]
            col = tile % TILE_Y + STEP_COL[direction]
            if 0 <= row < rows and 0 <= col < TILE_Y and keep(tile):
                found.append((tile, row * TILE_Y + col, direction))
        return found

    groups = [
        pairs_of(4, lambda t: t % 2 == 1) + pairs_of(3, lambda t: t % 2 == 0),
        pairs_of(4, lambda t: t % 2 == 0) + pairs_of(3, lambda t: t % 2 == 1),
    ]
    for direction in (0, 7, 1, 6, 2, 5):
        pairs = pairs_of(direction)
        for group in groups[2:]:
            sources = {p[0] for p in group}
            targets = {p[1] for p in group}
            if all(p[0] not in sources and p[1] not in targets for p in pairs):
                group.extend(pairs)
                break
        else:
            groups.append(pairs)
    groups = [g for g in groups if g]
    trash = block_count + 8 * slot_count + 1
    plan = np.zeros((len(groups), 2, tile_count), np.int32)
    plan[:, 1] = trash
    for index, group in enumerate(groups):
        for source, target, direction in group:
            plan[index, 0, source] = direction
            plan[index, 1, target] = block_count + (7 - direction) * slot_count
    return [[(s, t) for s, t, _ in g] for g in groups], plan


def here(values):
    me = lax.axis_index("tile")
    common = int(np.bincount(values).argmax())
    found = jnp.int32(common)
    for tile, value in enumerate(values):
        if value != common:
            found = jnp.where(me == tile, jnp.int32(int(value)), found)
    return found


def pack_kernel(plan, lists_ref, *refs):
    count = plan.shape[0]
    sources, refs = refs[:4], refs[4:]
    out_refs, copied, sems = refs[:count], refs[count:-1], refs[-1]
    copies = [
        pltpu.make_async_copy(source, target, sems.at[index])
        for index, (source, target) in enumerate(zip(sources, copied))
    ]
    for copy in copies:
        copy.start()
    pre_ref, feat_ref = copied[:2]
    copies[0].wait()
    copies[1].wait()
    last = pre_ref.shape[1] // 128 - 1
    for index, out_ref in enumerate(out_refs):
        direction = here(plan[index, 0])
        for slot in range(out_ref.shape[1]):
            block = jnp.minimum(lists_ref[0, direction, slot], last)
            lanes = pl.ds(pl.multiple_of(block * 128, 128), 128)
            out_ref[0, slot] = jnp.maximum(pre_ref[:, lanes], 0)
            out_ref[1, slot] = feat_ref[:, lanes]
    copies[2].wait()
    copies[3].wait()


def pack(lists, plan, *sources):
    shape = struct((2, lists.shape[2], sources[0].shape[0], 128), BF16)
    result = call(
        functools.partial(pack_kernel, plan),
        "pack_sends",
        [shape] * plan.shape[0] + [struct(s.shape, s.dtype) for s in sources],
        "SHHHH",
        (lists, *sources),
        [pltpu.SemaphoreType.DMA((4,))],
    )
    return result[: plan.shape[0]], result[plan.shape[0] :]


def gather_full(parts, full):
    me = lax.axis_index("chan")
    width = parts[0].shape[0]
    for step, part in enumerate(parts):
        full[pl.ds(pl.multiple_of((me ^ step) * width, 16), width), :] = part[...]


def partial_kernel(plan, riders, pin_ref, weight_ref, *refs):
    group_count = plan.shape[0]
    parts, refs = refs[:4], refs[4:]
    ride_refs, refs = refs[: len(riders)], refs[len(riders) :]
    local_ref = refs[0]
    back_refs = refs[1 : 1 + group_count]
    full, even_product, odd_product, even, odd = refs[1 + group_count :]
    offset_count, block_count = pin_ref.shape[1:]
    width = local_ref.shape[1]
    gather_full(parts, full)
    even[...] = jnp.zeros_like(even)
    odd[...] = jnp.zeros_like(odd)

    def multiply(turn, product):
        lanes = pl.ds(pl.multiple_of(turn * 256, 256), 256)
        product[...] = jnp.dot(weight_ref[...], full[:, lanes], preferred_element_type=F32)

    def land(turn, product):
        for offset in range(offset_count):
            for half, total in enumerate((even, odd)):
                entry = pin_ref[0, offset, turn * 2 + half]
                total[entry] += product[
                    offset * width : (offset + 1) * width, half * 128 : (half + 1) * 128
                ]

    turns = block_count // 2
    multiply(0, even_product)

    def two_turns(step, _):
        multiply(2 * step + 1, odd_product)
        land(2 * step, even_product)
        multiply(jnp.minimum(2 * step + 2, turns - 1), even_product)
        land(2 * step + 1, odd_product)
        return 0

    lax.fori_loop(0, turns // 2, two_turns, 0)
    local_ref[...] = even[:block_count] + odd[:block_count]
    for index, back_ref in enumerate(back_refs):
        base = here(plan[index, 1])
        for slot in range(back_ref.shape[1]):
            back_ref[0, slot] = (even[base + slot] + odd[base + slot]).astype(BF16)
    for index, ride_ref in zip(riders, ride_refs):
        back_refs[index][1:] = ride_ref[...]


def partial_sums(pin, plan, parts, weight, slot_count, riders=(), rides=()):
    width, voxels = parts[0].shape
    offset_count, block_count = pin.shape[1:]
    entries = block_count + 9 * slot_count + 1
    outs = [struct((block_count, width, 128), F32)]
    for group in range(plan.shape[0]):
        outs.append(struct((3 if group in riders else 1, slot_count, width, 128), BF16))
    flat = weight.reshape(offset_count * width, 4 * width)
    result = call(
        functools.partial(partial_kernel, plan, riders),
        "partial_sums",
        outs,
        "S",
        (pin, flat, *parts, *rides),
        [
            VMEM((4 * width, voxels), BF16),
            VMEM((offset_count * width, 256), F32),
            VMEM((offset_count * width, 256), F32),
            VMEM((entries, width, 128), F32),
            VMEM((entries, width, 128), F32),
        ],
        flops=2 * weight.size * voxels,
        vmem_mib=12,
    )
    return result[0], result[1:]


def packed_rows(rows, tile_count):
    step = 8 * tile_count
    return -(-(rows + rows // 2) // step) * step


def weight_kernel(plan, which, factor, pieces, pin_ref, own_ref, *refs):
    parts, refs = refs[:4], refs[4:]
    ghost_refs, refs = refs[: plan.shape[0]], refs[plan.shape[0] :]
    piece_refs, refs = refs[:pieces], refs[pieces:]
    full, extended, gathered, wide, tall = refs
    offset_count, block_count = pin_ref.shape[1:]
    width = own_ref.shape[0]
    gather_full(parts, full)
    for block in range(block_count):
        value = own_ref[:, block * 128 : (block + 1) * 128]
        extended[block] = jnp.maximum(value, 0) if which == 0 else value
    for index, ghost_ref in enumerate(ghost_refs):
        base = here(plan[index, 1])
        for slot in range(ghost_ref.shape[1]):
            extended[base + slot] = ghost_ref[ghost_ref.shape[0] - 2 + which, slot]
    empty = block_count + 8 * ghost_refs[0].shape[1]
    extended[empty] = jnp.zeros_like(extended[empty])
    chunk = gathered.shape[0] // width

    def some_offsets(turn, _):
        for step in range(chunk):
            for block in range(block_count):
                entry = pin_ref[0, turn * chunk + step, block]
                gathered[step * width : (step + 1) * width, block * 128 : (block + 1) * 128] = (
                    extended[entry]
                )
        grads = lax.dot_general(
            gathered[...], full[...], (((1,), (1,)), ((), ())), preferred_element_type=F32
        )
        rows = chunk * width
        wide[pl.ds(pl.multiple_of(turn * rows, 16), rows), : grads.shape[1]] = grads * factor
        return 0

    lax.fori_loop(0, offset_count // chunk, some_offsets, 0)
    rows, half = wide.shape[0], wide.shape[0] // 2
    tall[:rows] = wide[:, :128]
    tall[rows : rows + half, :64] = wide[:half, 128:192]
    tall[rows : rows + half, 64:] = wide[half:, 128:192]
    if tall.shape[0] > rows + half:
        tall[rows + half :] = jnp.zeros((tall.shape[0] - rows - half, 128), F32)
    split = tall.shape[0] // pieces
    mine = exchange_bit(0) if pieces == 2 else 2 * exchange_bit(0) + exchange_bit(1)
    for index, piece_ref in enumerate(piece_refs):
        piece = tall[pl.ds(pl.multiple_of((mine ^ index) * split, 8), split), :]
        piece_ref[...] = piece.astype(piece_ref.dtype)


def weight_sums(pin, plan, parts, own, ghosts, which, factor, tile_count, pieces):
    width, voxels = own.shape
    offset_count, block_count = pin.shape[1:]
    slot_count = ghosts[0].shape[1]
    entries = block_count + 9 * slot_count + 1
    chunk = 9 if offset_count % 9 == 0 else 1
    rows = offset_count * width
    tall = packed_rows(rows, tile_count)
    shape = (tall // pieces, 128)
    return call(
        functools.partial(weight_kernel, plan, which, factor, pieces),
        "weight_sums",
        [struct(shape, F32)] + [struct(shape, BF16)] * (pieces - 1),
        "S",
        (pin, own, *parts, *ghosts),
        [
            VMEM((4 * width, voxels), BF16),
            VMEM((entries, width, 128), BF16),
            VMEM((chunk * width, voxels), BF16),
            VMEM((rows, 256), F32),
            VMEM((tall, 128), F32),
        ],
        flops=2 * rows * 4 * width * voxels,
        vmem_mib=14,
    )


def settle_kernel(plan, first, lists_ref, other_ref, local_ref, *refs):
    *back_refs, out_ref, total = refs
    block_count = local_ref.shape[0]
    total[:block_count] = local_ref[...]
    for index, back_ref in enumerate(back_refs):
        direction = here(plan[index, 0])
        for slot in range(back_ref.shape[1]):
            block = lists_ref[0, direction, slot]
            total[block] += back_ref[0, slot].astype(F32)
    for block in range(block_count):
        lanes = slice(block * 128, (block + 1) * 128)
        other = other_ref[:, lanes].astype(F32)
        if first:
            value = jnp.where(other > 0, total[block], 0.0)
        else:
            value = other + total[block]
        out_ref[:, lanes] = value.astype(BF16)


def settle(first, lists, plan, local, other, backs):
    block_count, width, _ = local.shape
    return call(
        functools.partial(settle_kernel, plan, first),
        "settle",
        [struct(other.shape, BF16)],
        "S",
        (lists, other, local, *backs),
        [VMEM((block_count + 1, width, 128), F32)],
        flops=local.size,
    )[0]


def exchange_dim(step):
    parity = lax.axis_index("chan") % 2
    if step < 2:
        return jnp.where(parity == 0, step, 1 - step)
    return step


def exchange_bit(step):
    return lax.shift_right_logical(lax.axis_index("tile"), exchange_dim(step)) & 1


def trade(value, *steps):
    tile_count = lax.axis_size("tile")
    chan_count = lax.axis_size("chan")
    pairs = []
    for tile in range(tile_count):
        for chan in range(chan_count):
            dims = [(1 - step if chan % 2 else step) if step < 2 else step for step in steps]
            other = tile ^ sum(1 << dim for dim in dims)
            pairs.append((tile * chan_count + chan, other * chan_count + chan))
    return lax.ppermute(value, ("tile", "chan"), pairs)


def halve_kernel(step, sources, *refs):
    *_, next_ref, send_ref = refs
    bit = exchange_bit(step)
    split = next_ref.shape[1]
    mine = pl.ds(pl.multiple_of(bit * split, 8), split)
    theirs = pl.ds(pl.multiple_of((1 - bit) * split, 8), split)
    for index, terms in enumerate(sources):
        views = [refs[term] if part is None else refs[term].at[part] for term, part in terms]
        next_ref[index] = sum(view[mine, :].astype(F32) for view in views)
        send_ref[index] = sum(view[theirs, :].astype(F32) for view in views).astype(BF16)


def halve(step, sources, *args):
    shape = (len(sources), args[0].shape[-2] // 2, 128)
    return call(
        functools.partial(halve_kernel, step, sources),
        "halve",
        [struct(shape, F32), struct(shape, BF16)],
        "",
        args,
        flops=2 * args[0].size,
    )


def merge_kernel(keep_ref, got_ref, other_ref, next_ref, send_ref):
    bit = exchange_bit(1)
    split = next_ref.shape[0]
    mine = pl.ds(pl.multiple_of(bit * split, 8), split)
    theirs = pl.ds(pl.multiple_of((1 - bit) * split, 8), split)
    next_ref[...] = keep_ref[mine, :] + got_ref[mine, :].astype(F32)
    send_ref[0] = (keep_ref[theirs, :] + got_ref[theirs, :].astype(F32)).astype(BF16)
    send_ref[1] = other_ref[...]


def merge(keep, got, other):
    return call(
        merge_kernel,
        "merge_sends",
        [struct(other.shape, F32), struct((2,) + other.shape, BF16)],
        "",
        (keep, got, other),
        flops=keep.size,
    )


def unpack_kernel(tile_count, *refs):
    quarters, out_hbm, (wide, tall, sems) = refs[:4], refs[4:6], refs[6:]
    steps = tile_count.bit_length() - 1
    count, _, chunk, _ = quarters[0].shape
    rows = wide.shape[1]
    half = rows // 2
    mine = 0
    for step in range(steps):
        mine = mine * 2 + exchange_bit(step)
    copies = []
    for part in range(2):
        for index in range(tile_count):
            place = pl.ds(pl.multiple_of((mine ^ index) * chunk, 8), chunk)
            tall[place, :] = quarters[index // count][index % count, part].astype(F32)
        for side in range(2):
            here_rows = slice(side * half, (side + 1) * half)
            wide[part, here_rows, :128] = tall[here_rows]
            wide[part, here_rows, 128:192] = tall[rows : rows + half, side * 64 : side * 64 + 64]
            copies.append(
                pltpu.make_async_copy(
                    wide.at[part, here_rows],
                    out_hbm[part].at[here_rows],
                    sems.at[2 * part + side],
                )
            )
            copies[-1].start()
    for copy in copies:
        copy.wait()


def unpack(quarters, rows, columns):
    tile_count = 4 * quarters[0].shape[0]
    return call(
        functools.partial(unpack_kernel, tile_count),
        "unpack_sums",
        [struct((rows, columns), F32)] * 2,
        "",
        quarters,
        [
            VMEM((2, rows, columns), F32),
            VMEM((tile_count * quarters[0].shape[2], 128), F32),
            pltpu.SemaphoreType.DMA((4,)),
        ],
        vmem_mib=8,
        out_space="H",
    )


def swap_part(value, bits):
    return lax.ppermute(value, "chan", [(i, i ^ bits) for i in range(4)])


def shards(features, pre_act, cotangent, weight_one, weight_two, send_list, pair_in, pair_out):
    tile_count = lax.axis_size("tile")
    width, voxels = features.shape
    offset_count, _, columns = weight_one.shape
    block_count = pair_out.shape[2]
    slot_count = send_list.shape[2]
    rows = offset_count * width
    steps = tile_count.bit_length() - 1
    pair_lists, plan = ghost_plan(tile_count, block_count, slot_count)
    factor = 1.0 / math.sqrt(tile_count * voxels)
    tie = lambda *values: lax.optimization_barrier(values)

    def give(values, lists):
        return [lax.ppermute(v, "tile", p) for v, p in zip(values, lists)]

    back_lists = [[(t, s) for s, t in p] for p in pair_lists]

    early = (3, 2)
    riders = [g for g in range(len(pair_lists)) if g not in early]

    far, near, last = (swap_part(cotangent, bits) for bits in (2, 1, 3))
    sends, here_now = pack(send_list, plan, pre_act, features, cotangent, weight_two)
    pre_act, features, cotangent, weight_two = here_now
    soon = give([sends[g] for g in early], [pair_lists[g] for g in early])
    cot_parts = (cotangent, near, far, last)
    local_two, backs = partial_sums(
        pair_in, plan, cot_parts, weight_two, slot_count, riders, [sends[g] for g in riders]
    )
    backs, soon = tie(give(backs, back_lists), soon)
    grad_pre = settle(True, send_list, plan, local_two, pre_act, backs)

    ghosts = list(backs)
    for group, ghost in zip(early, soon):
        ghosts[group] = ghost
    far, near = swap_part(grad_pre, 2), swap_part(grad_pre, 1)
    keep_two, send = weight_sums(
        pair_in, plan, cot_parts, pre_act, ghosts, 0, factor, tile_count, 2
    )
    got_two = trade(send, 0)
    far, near, sent = tie(far, near, send)
    pre_parts = (grad_pre, near, far, swap_part(far, 1))
    keep_one, across_one, across_zero, across_both = weight_sums(
        pair_in, plan, pre_parts, features, ghosts, 1, factor, tile_count, 4
    )
    got_two, across_one = tie(got_two, across_one)
    got_zero, got_both = trade(across_zero, 0), trade(across_both, 0, 1)
    keep_two, send = merge(keep_two, got_two, across_one)
    got_one = trade(send, 1)
    pre_parts, keep_one = tie(pre_parts, keep_one)
    local_one, backs = partial_sums(pair_in, plan, pre_parts, weight_one, slot_count)
    shares = [[0, 1], [3], [2] + list(range(4, len(backs)))]
    returned = [None] * len(backs)

    def beside(value, step):
        share = shares.pop(0) if shares else []
        value, mine = tie(value, [backs[g] for g in share])
        got, landed = tie(trade(value, step), give(mine, [back_lists[g] for g in share]))
        for group, back in zip(share, landed):
            returned[group] = back
        return got

    arrived = (keep_two, got_one, keep_one, got_zero, got_both)
    sources = (((0, None), (1, 0)), ((2, None), (1, 1), (3, None), (4, None)))
    for step in range(2, steps):
        keep, send = halve(step, sources, *arrived)
        got = beside(send, step)
        arrived, sources = (keep, got), tuple(((0, part), (1, part)) for part in range(2))
    chunk = (keep + got.astype(F32)).astype(BF16)[None]
    for step in reversed(range(2, steps)):
        got = beside(chunk, step)
        chunk = jnp.concatenate([chunk, got], axis=0)
    share = sum(shares, [])
    chunk, mine = tie(chunk, [backs[g] for g in share])
    quarters = (chunk, trade(chunk, 1), trade(chunk, 0), trade(chunk, 0, 1))
    for group, back in zip(share, give(mine, [back_lists[g] for g in share])):
        returned[group] = back
    grad_features = settle(False, send_list, plan, local_one, cotangent, returned)
    sum_two, sum_one = unpack(quarters, rows, columns)
    shape = (offset_count, width, columns)
    return grad_features, sum_one.reshape(shape), sum_two.reshape(shape)


def solution(mesh):
    return jax.shard_map(
        shards,
        mesh=mesh,
        in_specs=(
            P("chan", "tile"),
            P("chan", "tile"),
            P("chan", "tile"),
            P(None, "chan", None),
            P(None, "chan", None),
            P("tile", None, None),
            P("tile", None, None),
            P("tile", None, None),
        ),
        out_specs=(P("chan", "tile"), P(None, "chan", None), P(None, "chan", None)),
        check_vma=False,
    )
```
